256 devices in a mesh: space: 32 (over y, z), spec: 8 (over x, core).
Axes of the slice: x: 4, y: 4, z: 8, core: 2. Of those that a mesh axis runs over, the one named last changes fastest.
Arguments:
- spectra: float32 [1296, 32768], P('spec', 'space'), may hold values from 0.1 to 2
- wet_mask: int32 [32768], P('space'), may hold values 0 or 1
- depth_class: int32 [32768], P('space'), may hold values from 0 to 31
- cg_table: float32 [36, 32], replicated, may hold values from 0.3 to 1
- neighbour: int32 [8, 32768], P(None, 'space'), may hold values from 0 to 3071, as said below
- edge_weight: float32 [8, 32768], P(None, 'space'), may hold values from 0.02 to 0.11
- edge_angle: float32 [8, 32768], P(None, 'space'), may hold values from -3.140625 to 3.140625
- send_list: int32 [32, 32, 64], P('space'), may hold values from 0 to 1023, as said below
- friction: float32 [32768], P('space'), may hold values from 0.2 to 1.5
- wind_dir: float32 [32768], P('space'), may hold values from -3.140625 to 3.140625
Outputs:
- spectra_next: float32 [1296, 32768], P('spec', 'space')
- energy: float32 [32768], P(('space', 'spec'))
The draws below stay inside these ranges and needn't reach their ends.
Inputs may be any that keep to these rules, and one draw needn't show every extreme that they name: `send_list`: block s sends only to blocks (s + 1), (s - 1), (s + 2), (s - 2) and (s + 16), all modulo 32; entries of any other pair, and entries at or past a pair's used count, are 0. The pair from each block s to block (s + 1) % 32 uses all 64 slots and its slot 0 holds node 1023. `neighbour`: A ghost entry 1024 + p * 64 + g has p among the blocks that send to the node's block and g below the count that block p uses towards it; an unused slot holds the node's own local index. Node 0 of every block b has slot 0 at ghost slot 63 from block (b - 1) % 32.
All inputs are finite; a program needn't handle non-finite values. No bound on the sum of `wet_mask` on one device may be relied on, other than what follows from the above.
Results may differ from the reference program's by a relative error of at most 0.000067.
Values sent between devices are 32-bit elements; how exact they have to be, the bound alone decides.
No kernel may reach another device: no remote copies, remote signals or barrier semaphores. Data moves between devices by JAX's collectives and lax.ppermute only.
A program may use at most 64 MiB of HBM per device.

```python
import math
import jax
import jax.numpy as jnp

NDIR = 36
NFREQ = 36
NCLASS = 32
MAXNB = 8
GHOST = 64
NODE_DEV = 1024
NODES = 32768
COMPS = 1296
N_SPACE = 32


def mesh_tables(key):
    space_count = N_SPACE
    subkeys = jax.random.split(jax.random.fold_in(key, 17), 6)
    source_block = jnp.arange(space_count, dtype=jnp.int32)[:, None]
    target_block = jnp.arange(space_count, dtype=jnp.int32)[None, :]
    distance = (target_block - source_block) % space_count
    peer_offsets = jnp.array([1, space_count - 1, 2, space_count - 2, space_count // 2], dtype=jnp.int32)
    is_peer = jnp.any(distance[:, :, None] == peer_offsets[None, None, :], axis=2)
    following = distance == 1
    counts = jax.random.randint(subkeys[0], (space_count, space_count), GHOST // 2, GHOST + 1)
    counts = jnp.where(following, GHOST, counts)
    counts = jnp.where(is_peer, counts, 0)
    slot_range = jnp.arange(GHOST, dtype=jnp.int32)
    send_table = jax.random.randint(subkeys[1], (space_count, space_count, GHOST), 0, NODE_DEV)
    send_table = jnp.where(slot_range[None, None, :] < counts[:, :, None], send_table, 0)
    send_table = jnp.where(following[:, :, None] & (slot_range == 0)[None, None, :], NODE_DEV - 1, send_table)
    node_total = NODE_DEV * space_count
    node_range = jnp.arange(node_total, dtype=jnp.int32)
    owner_block = node_range // NODE_DEV
    local_index = node_range % NODE_DEV
    category = jax.random.randint(subkeys[2], (MAXNB, node_total), 0, 20)
    offset_pick = jax.random.randint(subkeys[3], (MAXNB, node_total), 0, 5)
    peer_block = (owner_block[None, :] + peer_offsets[offset_pick]) % space_count
    pair_count = counts[peer_block, jnp.broadcast_to(owner_block[None, :], (MAXNB, node_total))]
    ghost_slot = jax.random.randint(subkeys[4], (MAXNB, node_total), 0, jnp.maximum(pair_count, 1))
    local_other = jax.random.randint(subkeys[5], (MAXNB, node_total), 0, NODE_DEV)
    neighbours = jnp.where(category < 3, NODE_DEV + peer_block * GHOST + ghost_slot, jnp.where(category < 15, local_other, jnp.broadcast_to(local_index[None, :], (MAXNB, node_total))))
    forced = NODE_DEV + (owner_block - 1) % space_count * GHOST + GHOST - 1
    first_row = jnp.where(local_index == 0, forced, neighbours[0])
    neighbours = neighbours.at[0].set(first_row)
    return (send_table.astype(jnp.int32), neighbours.astype(jnp.int32))


def draw_send_list(key, part):
    return mesh_tables(key)[0]


def draw_neighbour(key, part):
    return mesh_tables(key)[1]


def with_ends(values, rng, least, high):
    longest = values.shape.index(max(values.shape))
    spots = []
    for shift in (0, 1):
        where = [jax.random.randint(jax.random.fold_in(rng, axis), (), 0, length) for axis, length in enumerate(values.shape)]
        where[longest] = (where[longest] + shift) % values.shape[longest]
        spots.append(tuple(where))
    return values.at[spots[0]].set(least).at[spots[1]].set(high)


def block_scale(rng, extent, cuts, least, largest):
    factor_of, own = 1.0, jax.random.fold_in(rng, 6)
    for axis_at, blocks in cuts:
        draws = jnp.exp(jax.random.uniform(jax.random.fold_in(own, axis_at), (blocks,), jnp.float32, least / len(cuts), largest / len(cuts)))
        factor_of = factor_of * jnp.repeat(draws, extent[axis_at] // blocks).reshape([-1 if axis == axis_at else 1 for axis in range(len(extent))])
    return factor_of


def setup_inputs(seed: int = 0) -> dict:
    arg_keys = jax.random.split(jax.random.key(seed), 11)
    spectra = jnp.clip(jnp.exp(math.log(2.0) - 2.9957323 * jax.random.uniform(arg_keys[0], (COMPS, NODES), jnp.float32) ** block_scale(arg_keys[0], (COMPS, NODES), ((0, 8), (1, 32)), -0.2, 0.2)), 0.1, 2.0)
    wet_mask = with_ends((jax.random.randint(arg_keys[1], (NODES,), 0, 5) < 4).astype(jnp.int32), jax.random.fold_in(arg_keys[1], 1), 0, 1)
    depth_class = with_ends(jax.random.randint(arg_keys[2], (NODES,), 0, NCLASS), jax.random.fold_in(arg_keys[2], 1), 0, NCLASS - 1).astype(jnp.int32)
    cg_table = jnp.clip(jnp.exp(jax.random.uniform(arg_keys[3], (NFREQ, NCLASS), jnp.float32, math.log(0.3), math.log(1.0))), 0.3, 1.0)
    neighbour = draw_neighbour(jax.random.fold_in(arg_keys[10], 71), 0)
    edge_weight = jnp.clip(jnp.exp(math.log(0.11) - 1.7047481 * jax.random.uniform(arg_keys[5], (MAXNB, NODES), jnp.float32) ** block_scale(arg_keys[5], (MAXNB, NODES), ((1, 32),), -0.2, 0.2)), 0.02, 0.11)
    edge_angle = jnp.clip(jax.random.uniform(arg_keys[6], (MAXNB, NODES), jnp.float32, -3.140625, 3.140625), -3.140625, 3.140625)
    send_list = draw_send_list(jax.random.fold_in(arg_keys[10], 71), 0)
    friction = jnp.clip(jnp.exp(math.log(1.5) - 2.014903 * jax.random.uniform(arg_keys[8], (NODES,), jnp.float32) ** block_scale(arg_keys[8], (NODES,), ((0, 32),), -0.2, 0.2)), 0.2, 1.5)
    wind_dir = jnp.clip(jax.random.uniform(arg_keys[9], (NODES,), jnp.float32, -3.140625, 3.140625), -3.140625, 3.140625)
    return {"spectra": spectra, "wet_mask": wet_mask, "depth_class": depth_class, "cg_table": cg_table, "neighbour": neighbour, "edge_weight": edge_weight, "edge_angle": edge_angle, "send_list": send_list, "friction": friction, "wind_dir": wind_dir}


def spectral_constants():
    level_index = jnp.arange(NFREQ, dtype=jnp.float32)
    frequency = 0.04 * jnp.exp(level_index * jnp.float32(math.log(1.1)))
    spread = 0.1 * frequency
    band_weight = spread / (NDIR * jnp.sum(spread))
    direction_angle = jnp.arange(NDIR, dtype=jnp.float32) * jnp.float32(2.0 * math.pi / NDIR)
    return frequency, band_weight, jnp.cos(direction_angle), jnp.sin(direction_angle)


def point_source(values, energy, moment, freq_col, cos_col, sin_col, friction_row, dir_row):
    top_freq = 0.04 * jnp.exp(jnp.float32(NFREQ - 1) * jnp.float32(math.log(1.1)))
    mean_freq = (moment + 4e-8) / (energy + 1e-6)
    steepness = energy * (mean_freq / 0.8) ** 4
    dissipation = (steepness ** 2)[None, :] * freq_col[:, None] / mean_freq[None, :]
    drive = cos_col[:, None] * jnp.cos(dir_row)[None, :] + sin_col[:, None] * jnp.sin(dir_row)[None, :]
    relative = freq_col / top_freq
    wind_input = 0.5 * jnp.maximum(4.0 * friction_row[None, :] * relative[:, None] * drive - 1.0, 0.0)
    return values * jnp.exp(0.25 * (wind_input - dissipation))


def reference(spectra, wet_mask, depth_class, cg_table, neighbour, edge_weight, edge_angle, send_list, friction, wind_dir):
    node_total = spectra.shape[1]
    comp_total = spectra.shape[0]
    extended = NODE_DEV + N_SPACE * GHOST
    wet_float = wet_mask.astype(jnp.float32)
    masked = spectra * wet_float[None, :]
    block_range = jnp.arange(N_SPACE, dtype=jnp.int32)
    ghost_global = block_range[None, :, None] * NODE_DEV + jnp.transpose(send_list, (1, 0, 2))
    own_global = block_range[:, None] * NODE_DEV + jnp.arange(NODE_DEV, dtype=jnp.int32)[None, :]
    lookup_table = jnp.concatenate([own_global, ghost_global.reshape(N_SPACE, N_SPACE * GHOST)], axis=1)
    owner_block = jnp.arange(node_total, dtype=jnp.int32) // NODE_DEV
    global_nb = lookup_table.reshape(-1)[owner_block[None, :] * extended + neighbour]
    frequency, band_weight, dir_cosine, dir_sine = spectral_constants()
    comp_range = jnp.arange(comp_total, dtype=jnp.int32)
    freq_index = comp_range // NDIR
    dir_index = comp_range % NDIR
    group_speed = cg_table[freq_index][:, depth_class]
    cos_col = dir_cosine[dir_index]
    sin_col = dir_sine[dir_index]
    accumulated = jnp.zeros_like(masked)
    for slot_index in range(MAXNB):
        alignment = cos_col[:, None] * jnp.cos(edge_angle[slot_index])[None, :] + sin_col[:, None] * jnp.sin(edge_angle[slot_index])[None, :]
        coefficient = group_speed * edge_weight[slot_index][None, :] * jnp.maximum(alignment, 0.0)
        accumulated = accumulated + coefficient * (masked[:, global_nb[slot_index]] - masked)
    advected = (masked + accumulated) * wet_float[None, :]
    freq_col = frequency[freq_index]
    weight_col = band_weight[freq_index]
    energy = jnp.sum(advected * weight_col[:, None], axis=0)
    moment = jnp.sum(advected * (weight_col * freq_col)[:, None], axis=0)
    spectra_next = point_source(advected, energy, moment, freq_col, cos_col, sin_col, friction, wind_dir)
    return spectra_next, energy
```

```python
import math

import numpy as np
import jax
import jax.numpy as jnp
from jax import lax
from jax.experimental import pallas as pl
from jax.experimental.pallas import tpu as pltpu
from jax.sharding import PartitionSpec as P

NDIR = 36
NFREQ = 36
GHOST = 64
LANES = 128
PACK = 88
OFFSETS = (1, 31, 2, 30, 16)
SCALE = 32767.5

_F = 0.04 * np.exp(np.arange(NFREQ) * math.log(1.1))
_KAPPA = float(0.1 / (NDIR * np.sum(0.1 * _F)))
_FTOP = float(_F[-1])


def _tables():
    angle = 2.0 * np.pi * (np.arange(72) % NDIR) / NDIR
    cosine = np.repeat(np.cos(angle)[:, None], LANES, 1)
    sine = np.repeat(np.sin(angle)[:, None], LANES, 1)
    freq = np.zeros((40, LANES))
    freq[:NFREQ] = _F[:, None]
    return np.concatenate([cosine, sine, freq]).astype(np.float32)


def lane_gather(values, index):
    return jnp.take_along_axis(values, index, axis=1, mode="promise_in_bounds")


def pick(blocks, index, bits):
    level = [lane_gather(block, index) for block in blocks]
    for bit in bits:
        level = [
            jnp.where(bit, level[i + 1], level[i]) if i + 1 < len(level) else level[i]
            for i in range(0, len(level), 2)
        ]
    return level[0]


def row8(row):
    return jnp.broadcast_to(row, (8, LANES))


def send_kernel(me_ref, x_ref, wet_ref, send_ref, out_ref):
    me = me_ref[0]
    rows = [send_ref[pl.ds((me + o) & 31, 1), :] for o in OFFSETS]
    lane = lax.broadcasted_iota(jnp.int32, (8, LANES), 1)
    low = lane < GHOST
    index = []
    for a, b in ((0, 1), (2, 3), (4, 4)):
        full = row8(jnp.concatenate([rows[a], rows[b]], axis=1))
        block = full >> 7
        index.append((full & 127, [(block & 1) == 1, (block & 2) == 2, (block & 4) == 4]))
    wet = [row8(wet_ref[b : b + 1, :].astype(jnp.float32)) for b in range(8)]

    def source(g):
        if g < 20:
            return [
                x_ref[8 * g : 8 * g + 8, LANES * b : LANES * b + LANES] * wet[b] for b in range(8)
            ]
        zero = jnp.zeros((6, LANES), jnp.float32)
        return [
            jnp.concatenate([x_ref[160:162, LANES * b : LANES * b + LANES], zero], axis=0) * wet[b]
            for b in range(8)
        ]

    for g in range(11):
        first = source(g)
        second = source(g + 11) if g < 10 else None
        for q in range(3):
            top = pick(first, *index[q])
            bottom = pick(second, *index[q]) if second is not None else jnp.zeros_like(top)
            if q < 2:
                out_ref[2 * q, 8 * g : 8 * g + 8, :] = jnp.where(low, top, pltpu.roll(bottom, 64, 1))
                out_ref[2 * q + 1, 8 * g : 8 * g + 8, :] = jnp.where(
                    low, pltpu.roll(top, 64, 1), bottom
                )
            else:
                out_ref[4, 8 * g : 8 * g + 8, :] = jnp.where(low, top, bottom)


def local_kernel(
    id_ref,
    x_ref,
    wet_ref,
    nb_ref,
    ew_ref,
    ea_ref,
    dc_ref,
    cg_ref,
    fr_ref,
    wd_ref,
    tab_ref,
    base_ref,
    gain_ref,
    xs_ref,
    wind_ref,
    fc_ref,
    geo_ref,
    code_ref,
    packed,
    cgx,
    wloc,
):
    me = id_ref[0]
    spec = id_ref[1]
    par = spec & 1
    first_freq = (9 * spec) >> 1
    sign = (1 - 2 * par).astype(jnp.float32)
    entry = nb_ref[...]
    ghost = entry >= 1024
    angle = ea_ref[...]
    weight = ew_ref[...] * (sign * (1.0 / SCALE))
    wc = weight * jnp.cos(angle)
    ws = weight * jnp.sin(angle)
    wloc[0] = jnp.where(ghost, 0.0, wc)
    wloc[1] = jnp.where(ghost, 0.0, ws)
    geo_ref[0] = jnp.where(ghost, wc, 0.0)
    geo_ref[1] = jnp.where(ghost, ws, 0.0)
    peer = (entry - 1024) >> 6
    off = (me - peer) & 31
    half = (off == 31) | (off == 30)
    block = jnp.where(off == 16, 2, jnp.where((off == 2) | (off == 30), 1, 0))
    code_ref[...] = (entry & 63) + jnp.where(half, 64, 0) + 128 * block
    cgpad = [None] * 5
    fpad = [None] * 5
    for j in range(5):
        line = cg_ref[pl.ds(first_freq + j, 1), :]
        cgpad[j] = row8(jnp.concatenate([line, line, line, line], axis=1))
        fpad[j] = row8(tab_ref[pl.ds(144 + first_freq + j, 1), :])
    for g in range(21):
        comp = lax.broadcasted_iota(jnp.int32, (8, LANES), 0) + 8 * g + 18 * par
        cv, fv = cgpad[0], fpad[0]
        for j in range(1, 5):
            if 8 * g + 7 + 18 >= 36 * j:
                later = comp >= 36 * j
                cv = jnp.where(later, cgpad[j], cv)
                fv = jnp.where(later, fpad[j], fv)
        cgx[8 * g : 8 * g + 8, :] = cv
        fc_ref[8 * g : 8 * g + 8, :] = fv
    for b in range(8):
        lanes = slice(LANES * b, LANES * b + LANES)
        wet = row8(wet_ref[b : b + 1, :].astype(jnp.float32)) * SCALE
        for g in range(20):
            xs_ref[8 * g : 8 * g + 8, lanes] = x_ref[8 * g : 8 * g + 8, lanes] * wet
        tail = jnp.concatenate([x_ref[160:162, lanes], jnp.zeros((6, LANES), jnp.float32)], axis=0)
        xs_ref[160:168, lanes] = tail * wet
        for g in range(11):
            top = (xs_ref[8 * g : 8 * g + 8, lanes] + 0.5).astype(jnp.int32) << 16
            if g < 10:
                top = top | (xs_ref[8 * g + 88 : 8 * g + 96, lanes] + 0.5).astype(jnp.int32)
            packed[8 * g : 8 * g + 8, lanes] = top

    def node_block(b, carry):
        lanes = pl.ds(pl.multiple_of(b * LANES, LANES), LANES)
        wet = row8(wet_ref[pl.ds(b, 1), :].astype(jnp.float32))
        cls = row8(dc_ref[pl.ds(b, 1), :])
        total = [jnp.zeros((8, LANES), jnp.float32) for _ in range(21)]
        for m in range(8):
            full = row8(nb_ref[m : m + 1, lanes])
            index = full & 127
            bits = [(full & 128) != 0, (full & 256) != 0, (full & 512) != 0]
            wc = row8(wloc[0, m : m + 1, lanes])
            ws = row8(wloc[1, m : m + 1, lanes])
            for g in range(11):
                word = pick(
                    [packed[8 * g : 8 * g + 8, LANES * s : LANES * s + LANES] for s in range(8)],
                    index,
                    bits,
                )
                for h, value in ((g, lax.shift_right_logical(word, 16)), (g + 11, word & 65535)):
                    if h > 20:
                        continue
                    r = 8 * (h % 9)
                    share = jnp.maximum(
                        tab_ref[r : r + 8, :] * wc + tab_ref[72 + r : 80 + r, :] * ws, 0.0
                    )
                    total[h] = total[h] + share * (
                        value.astype(jnp.float32) - xs_ref[8 * h : 8 * h + 8, lanes]
                    )
        drive4 = row8(fr_ref[pl.ds(b, 1), :]) * (sign * 4.0 / _FTOP)
        heading = row8(wd_ref[pl.ds(b, 1), :])
        dcos = drive4 * jnp.cos(heading)
        dsin = drive4 * jnp.sin(heading)
        for g in range(21):
            rows = slice(8 * g, 8 * g + 8)
            gain = wet * lane_gather(cgx[rows, :], cls)
            gain_ref[rows, lanes] = gain
            base_ref[rows, lanes] = xs_ref[rows, lanes] * (1.0 / SCALE) + gain * total[g]
            r = 8 * (g % 9)
            drive = tab_ref[r : r + 8, :] * dcos + tab_ref[72 + r : 80 + r, :] * dsin
            wind_ref[rows, lanes] = 0.125 * jnp.maximum(fc_ref[rows, :] * drive - 1.0, 0.0)
        return carry

    lax.fori_loop(0, 8, node_block, 0)


def ghost_kernel(
    g0, g1, g2, g3, g4, base_ref, gain_ref, xs_ref, fc_ref, geo_ref, code_ref, tab_ref, adv_ref,
    sums_ref, packed
):
    low = lax.broadcasted_iota(jnp.int32, (8, LANES), 1) < GHOST
    for g in range(11):
        rows = slice(8 * g, 8 * g + 8)
        whole = [(ref[rows, :] * SCALE + 0.5).astype(jnp.int32) for ref in (g0, g1, g2, g3, g4)]
        for q in range(3):
            a = whole[2 * q]
            word = (a << 16) | pltpu.roll(a, 64, 1)
            if q < 2:
                c = whole[2 * q + 1]
                word = jnp.where(low, word, (pltpu.roll(c, 64, 1) << 16) | c)
            packed[rows, LANES * q : LANES * q + LANES] = word

    def node_block(b, carry):
        lanes = pl.ds(pl.multiple_of(b * LANES, LANES), LANES)
        total = [jnp.zeros((8, LANES), jnp.float32) for _ in range(21)]
        for m in range(8):
            full = row8(code_ref[m : m + 1, lanes])
            index = full & 127
            bits = [(full & 128) != 0, (full & 256) != 0]
            wc = row8(geo_ref[0, m : m + 1, lanes])
            ws = row8(geo_ref[1, m : m + 1, lanes])
            for g in range(11):
                word = pick(
                    [packed[8 * g : 8 * g + 8, LANES * s : LANES * s + LANES] for s in range(3)],
                    index,
                    bits,
                )
                for h, value in ((g, lax.shift_right_logical(word, 16)), (g + 11, word & 65535)):
                    if h > 20:
                        continue
                    r = 8 * (h % 9)
                    share = jnp.maximum(
                        tab_ref[r : r + 8, :] * wc + tab_ref[72 + r : 80 + r, :] * ws, 0.0
                    )
                    total[h] = total[h] + share * (
                        value.astype(jnp.float32) - xs_ref[8 * h : 8 * h + 8, lanes]
                    )
        energy = jnp.zeros((8, LANES), jnp.float32)
        moment = jnp.zeros((8, LANES), jnp.float32)
        for g in range(21):
            rows = slice(8 * g, 8 * g + 8)
            adv = base_ref[rows, lanes] + gain_ref[rows, lanes] * total[g]
            adv_ref[rows, lanes] = adv
            freq = fc_ref[rows, :]
            term = freq * adv
            energy = energy + term
            moment = moment + freq * term
        erow = jnp.sum(energy, axis=0, keepdims=True) * _KAPPA
        mrow = jnp.sum(moment, axis=0, keepdims=True) * _KAPPA
        for r in range(8):
            sums_ref[r, pl.ds(b, 1), :] = erow
            sums_ref[r, pl.ds(b + 8, 1), :] = mrow
        return carry

    lax.fori_loop(0, 8, node_block, 0)


def source_kernel(id_ref, sums_ref, adv_ref, wind_ref, fc_ref, out_ref, energy_ref, damp):
    spec = id_ref[1]
    total = sums_ref[0]
    for r in range(1, 8):
        total = total + sums_ref[r]
    energy = total[0:8]
    moment = total[8:16]
    mean = (moment + 4e-8) / (energy + 1e-6)
    scaled = mean / 0.8
    steep = energy * (scaled * scaled) * (scaled * scaled)
    damp[...] = (0.25 * steep) * steep / mean
    mine = lax.broadcasted_iota(jnp.int32, (8, LANES), 0) == spec
    energy_ref[...] = jnp.sum(jnp.where(mine, energy, 0.0), axis=0, keepdims=True)
    for b in range(8):
        lanes = slice(LANES * b, LANES * b + LANES)
        rate = row8(damp[b : b + 1, :])
        for g in range(21):
            n = 8 if g < 20 else 2
            rows = slice(8 * g, 8 * g + 8)
            value = adv_ref[rows, lanes] * jnp.exp(wind_ref[rows, lanes] - rate * fc_ref[rows, :])
            out_ref[8 * g : 8 * g + n, lanes] = value[0:n]


SMEM = pl.BlockSpec(memory_space=pltpu.SMEM)
VMEM = pl.BlockSpec(memory_space=pltpu.VMEM)
F32 = jnp.float32


def shape(*dims, dtype=jnp.float32):
    return jax.ShapeDtypeStruct(dims, dtype)


def cost(flops, size):
    return pl.CostEstimate(flops=flops, bytes_accessed=size, transcendentals=0)


LIMIT = pltpu.CompilerParams(vmem_limit_bytes=32 << 20)


def per_device(
    spectra,
    wet_mask,
    depth_class,
    cg_table,
    neighbour,
    edge_weight,
    edge_angle,
    send_list,
    friction,
    wind_dir,
):
    me = lax.axis_index("space")
    spec = lax.axis_index("spec")
    ids = jnp.stack([me, spec]).astype(jnp.int32)
    wet = wet_mask.reshape(8, LANES)
    table = jnp.asarray(_tables())
    outgoing = pl.pallas_call(
        send_kernel,
        out_shape=shape(5, PACK, LANES),
        in_specs=[SMEM, VMEM, VMEM, VMEM],
        out_specs=VMEM,
        compiler_params=LIMIT,
        name="send_pack",
    )(ids, spectra, wet, send_list[0])
    ghosts = [
        lax.ppermute(outgoing[k], "space", [(i, (i + o) % 32) for i in range(32)])
        for k, o in enumerate(OFFSETS)
    ]
    base, gain, scaled, wind, freq, geo, code = pl.pallas_call(
        local_kernel,
        out_shape=(
            shape(168, 1024),
            shape(168, 1024),
            shape(168, 1024),
            shape(168, 1024),
            shape(168, LANES),
            shape(2, 8, 1024),
            shape(8, 1024, dtype=jnp.int32),
        ),
        in_specs=[SMEM] + [VMEM] * 10,
        out_specs=(VMEM,) * 7,
        scratch_shapes=[
            pltpu.VMEM((PACK, 1024), jnp.int32),
            pltpu.VMEM((168, LANES), F32),
            pltpu.VMEM((2, 8, 1024), F32),
        ],
        compiler_params=LIMIT,
        cost_estimate=cost(20_000_000, 4_000_000),
        name="local_slots",
    )(
        ids,
        spectra,
        wet,
        neighbour,
        edge_weight,
        edge_angle,
        depth_class.reshape(8, LANES),
        cg_table,
        friction.reshape(8, LANES),
        wind_dir.reshape(8, LANES),
        table,
    )
    advected, sums = pl.pallas_call(
        ghost_kernel,
        out_shape=(shape(168, 1024), shape(8, 16, LANES)),
        in_specs=[VMEM] * 12,
        out_specs=(VMEM,) * 2,
        scratch_shapes=[pltpu.VMEM((PACK, 3 * LANES), jnp.int32)],
        compiler_params=LIMIT,
        name="ghost_slots",
    )(*ghosts, base, gain, scaled, freq, geo, code, table)
    parts = lax.all_to_all(sums, "spec", split_axis=0, concat_axis=0, tiled=True)
    result, energy = pl.pallas_call(
        source_kernel,
        out_shape=(shape(162, 1024), shape(1, LANES)),
        in_specs=[SMEM] + [VMEM] * 4,
        out_specs=(VMEM,) * 2,
        scratch_shapes=[pltpu.VMEM((8, LANES), F32)],
        compiler_params=LIMIT,
        name="source",
    )(ids, parts, advected, wind, freq)
    return result, energy.reshape(LANES)


def solution(mesh):
    placed = (
        P("spec", "space"),
        P("space"),
        P("space"),
        P(),
        P(None, "space"),
        P(None, "space"),
        P(None, "space"),
        P("space", None, None),
        P("space"),
        P("space"),
    )
    return jax.shard_map(
        per_device,
        mesh=mesh,
        in_specs=placed,
        out_specs=(P("spec", "space"), P(("space", "spec"))),
        check_vma=False,
    )
```

```python
import math

import numpy as np
import jax
import jax.numpy as jnp
from jax import lax
from jax.experimental import pallas as pl
from jax.experimental.pallas import tpu as pltpu
from jax.sharding import PartitionSpec as P

NDIR = 36
NFREQ = 36
GHOST = 64
LANES = 128
PACK = 88
OFFSETS = (1, 31, 2, 30, 16)
SCALE = 32767.5

_F = 0.04 * np.exp(np.arange(NFREQ) * math.log(1.1))
_KAPPA = float(0.1 / (NDIR * np.sum(0.1 * _F)))
_FTOP = float(_F[-1])


def _tables():
    angle = 2.0 * np.pi * (np.arange(72) % NDIR) / NDIR
    cosine = np.repeat(np.cos(angle)[:, None], LANES, 1)
    sine = np.repeat(np.sin(angle)[:, None], LANES, 1)
    freq = np.zeros((40, LANES))
    freq[:NFREQ] = _F[:, None]
    return np.concatenate([cosine, sine, freq]).astype(np.float32)


def lane_gather(values, index):
    return jnp.take_along_axis(values, index, axis=1, mode="promise_in_bounds")


def pick(blocks, index, bits):
    level = [lane_gather(block, index) for block in blocks]
    for bit in bits:
        level = [
            jnp.where(bit, level[i + 1], level[i]) if i + 1 < len(level) else level[i]
            for i in range(0, len(level), 2)
        ]
    return level[0]


def row8(row):
    return jnp.broadcast_to(row, (8, LANES))


def turn(angle):
    h = 0.5 * angle
    t = h * h
    s = h * (
        1.0
        + t
        * (
            -1.6666666666e-1
            + t * (8.3333331e-3 + t * (-1.98412e-4 + t * (2.75567e-6 - t * 2.4700e-8)))
        )
    )
    c = 1.0 + t * (
        -0.5
        + t * (4.16666664e-2 + t * (-1.3888883e-3 + t * (2.480065e-5 + t * (-2.75358e-7 + t * 2.065e-9))))
    )
    return 1.0 - 2.0 * s * s, 2.0 * s * c


CHUNKS = ((0, 6), (6, 11))


def send_kernel(
    x_hbm, plan_ref, o0, o1, o2, o3, o4, masked_ref, packed_ref, x_ref, code_ref,
    words_ref, sem
):
    outs = (o0, o1, o2, o3, o4)
    copies = []
    for i, (first, last) in enumerate(CHUNKS):
        for j, base in enumerate((0, PACK)):
            rows = pl.ds(base + 8 * first, min(8 * last + base, 162) - base - 8 * first)
            copies.append(
                pltpu.make_async_copy(x_hbm.at[rows, :], x_ref.at[rows, :], sem.at[2 * i + j])
            )
    for copy in copies:
        copy.start()
    me = lax.axis_index("space")
    lane = lax.broadcasted_iota(jnp.int32, (8, LANES), 1)
    low = lane < GHOST
    rows = [plan_ref[pl.ds(8 + ((me + o) & 31), 1), 0:GHOST] for o in OFFSETS]
    for q, (a, b) in enumerate(((0, 1), (2, 3), (4, 4))):
        code_ref[q] = row8(jnp.concatenate([rows[a], rows[b]], axis=1))
    wet = [row8(plan_ref[b : b + 1, :].astype(jnp.float32)) for b in range(8)]

    def load(g, b):
        lanes = slice(LANES * b, LANES * b + LANES)
        if g < 20:
            value = x_ref[8 * g : 8 * g + 8, lanes] * wet[b]
        else:
            zero = jnp.zeros((6, LANES), jnp.float32)
            value = jnp.concatenate([x_ref[160:162, lanes], zero], axis=0) * wet[b]
        masked_ref[8 * g : 8 * g + 8, lanes] = value
        return (value * SCALE + 0.5).astype(jnp.int32)

    for i, (first, last) in enumerate(CHUNKS):
        copies[2 * i].wait()
        copies[2 * i + 1].wait()
        for g in range(first, last):
            for b in range(8):
                word = load(g, b) << 16
                if g < 10:
                    word = word | load(g + 11, b)
                packed_ref[8 * g : 8 * g + 8, LANES * b : LANES * b + LANES] = word

    def gather(q, carry):
        full = code_ref[q]
        index = full & 127
        bits = [(full & (128 << i)) != 0 for i in range(3)]
        for g in range(11):
            rows = slice(8 * g, 8 * g + 8)
            words_ref[q, rows, :] = pick(
                [packed_ref[rows, LANES * b : LANES * b + LANES] for b in range(8)], index, bits
            )
        return carry

    lax.fori_loop(0, 3, gather, 0)
    for q in range(3):
        for g in range(11):
            rows = slice(8 * g, 8 * g + 8)
            word = words_ref[q, rows, :]
            top = lax.shift_right_logical(word, 16).astype(jnp.float32)
            bottom = (word & 65535).astype(jnp.float32)
            if q < 2:
                outs[2 * q][rows, :] = jnp.where(low, top, pltpu.roll(bottom, 64, 1))
                outs[2 * q + 1][rows, :] = jnp.where(low, pltpu.roll(top, 64, 1), bottom)
            else:
                outs[4][rows, :] = jnp.where(low, top, bottom)


def slots(packed, blocks, code, geo, tab_ref, lanes, bit_count):
    total = [None] * 21
    shares = [None] * 9
    for m in range(8):
        full = row8(code[m : m + 1, lanes])
        index = full & 127
        bits = [(full & (128 << i)) != 0 for i in range(bit_count)]
        wc = row8(geo[0, m : m + 1, lanes])
        ws = row8(geo[1, m : m + 1, lanes])
        share = [
            jnp.maximum(
                tab_ref[8 * r : 8 * r + 8, :] * wc + tab_ref[72 + 8 * r : 80 + 8 * r, :] * ws, 0.0
            )
            for r in range(9)
        ]
        shares = [s if t is None else t + s for t, s in zip(shares, share)]
        for g in range(11):
            word = pick(
                [packed[8 * g : 8 * g + 8, LANES * s : LANES * s + LANES] for s in range(blocks)],
                index,
                bits,
            )
            for h, value in ((g, lax.shift_right_logical(word, 16)), (g + 11, word & 65535)):
                if h < 21:
                    term = share[h % 9] * value.astype(jnp.float32)
                    total[h] = term if total[h] is None else total[h] + term
    return total, shares


def local_kernel(
    x_ref,
    packed,
    wet_ref,
    nb_ref,
    ew_ref,
    ea_ref,
    dc_ref,
    cg_ref,
    fr_ref,
    wd_ref,
    tab_ref,
    base_ref,
    gain_ref,
    wind_ref,
    fc_ref,
    geo_ref,
    code_ref,
    cgx,
    wloc,
    drive_ref,
):
    me = lax.axis_index("space")
    spec = lax.axis_index("spec")
    par = spec & 1
    first_freq = (9 * spec) >> 1
    sign = (1 - 2 * par).astype(jnp.float32)
    entry = nb_ref[...]
    ghost = entry >= 1024
    weight = ew_ref[...] * sign
    cosine, sine = turn(ea_ref[...])
    wc = weight * cosine
    ws = weight * sine
    wloc[0] = jnp.where(ghost, 0.0, wc)
    wloc[1] = jnp.where(ghost, 0.0, ws)
    geo_ref[0] = jnp.where(ghost, wc, 0.0)
    geo_ref[1] = jnp.where(ghost, ws, 0.0)
    peer = (entry - 1024) >> 6
    off = (me - peer) & 31
    half = (off == 31) | (off == 30)
    block = jnp.where(off == 16, 2, jnp.where((off == 2) | (off == 30), 1, 0))
    code_ref[...] = (entry & 63) + jnp.where(half, 64, 0) + 128 * block
    drive4 = fr_ref[...] * (sign * 4.0 / _FTOP)
    cosine, sine = turn(wd_ref[...])
    drive_ref[0] = drive4 * cosine
    drive_ref[1] = drive4 * sine
    cgpad = [None] * 5
    fpad = [None] * 5
    for j in range(5):
        line = cg_ref[pl.ds(first_freq + j, 1), :]
        cgpad[j] = row8(jnp.concatenate([line, line, line, line], axis=1))
        fpad[j] = row8(tab_ref[pl.ds(144 + first_freq + j, 1), :])
    for g in range(21):
        comp = lax.broadcasted_iota(jnp.int32, (8, LANES), 0) + 8 * g + 18 * par
        cv, fv = cgpad[0], fpad[0]
        for j in range(1, 5):
            if 8 * g + 7 + 18 >= 36 * j:
                later = comp >= 36 * j
                cv = jnp.where(later, cgpad[j], cv)
                fv = jnp.where(later, fpad[j], fv)
        cgx[8 * g : 8 * g + 8, :] = cv
        fc_ref[8 * g : 8 * g + 8, :] = fv

    def node_block(b, carry):
        lanes = pl.ds(pl.multiple_of(b * LANES, LANES), LANES)
        wet = row8(wet_ref[pl.ds(b, 1), :].astype(jnp.float32))
        cls = row8(dc_ref[pl.ds(b, 1), :])
        total, shares = slots(packed, 8, nb_ref, wloc, tab_ref, lanes, 3)
        dcos = row8(drive_ref[0, pl.ds(b, 1), :])
        dsin = row8(drive_ref[1, pl.ds(b, 1), :])
        for g in range(21):
            rows = slice(8 * g, 8 * g + 8)
            gain = wet * lane_gather(cgx[rows, :], cls)
            gain_ref[rows, lanes] = gain
            x = x_ref[rows, lanes]
            base_ref[rows, lanes] = x + gain * (total[g] * (1.0 / SCALE) - x * shares[g % 9])
            r = 8 * (g % 9)
            drive = tab_ref[r : r + 8, :] * dcos + tab_ref[72 + r : 80 + r, :] * dsin
            wind_ref[rows, lanes] = 0.125 * jnp.maximum(fc_ref[rows, :] * drive - 1.0, 0.0)
        return carry

    lax.fori_loop(0, 8, node_block, 0, unroll=2)


def ghost_kernel(
    g0, g1, g2, g3, g4, x_ref, base_ref, gain_ref, fc_ref, geo_ref, code_ref, tab_ref, adv_ref,
    sums_ref, packed
):
    low = lax.broadcasted_iota(jnp.int32, (8, LANES), 1) < GHOST
    for g in range(11):
        rows = slice(8 * g, 8 * g + 8)
        whole = [ref[rows, :].astype(jnp.int32) for ref in (g0, g1, g2, g3, g4)]
        for q in range(3):
            a = whole[2 * q]
            word = (a << 16) | pltpu.roll(a, 64, 1)
            if q < 2:
                c = whole[2 * q + 1]
                word = jnp.where(low, word, (pltpu.roll(c, 64, 1) << 16) | c)
            packed[rows, LANES * q : LANES * q + LANES] = word

    def node_block(b, carry):
        lanes = pl.ds(pl.multiple_of(b * LANES, LANES), LANES)
        total, shares = slots(packed, 3, code_ref, geo_ref, tab_ref, lanes, 2)
        energy = jnp.zeros((8, LANES), jnp.float32)
        moment = jnp.zeros((8, LANES), jnp.float32)
        for g in range(21):
            rows = slice(8 * g, 8 * g + 8)
            inflow = total[g] * (1.0 / SCALE) - x_ref[rows, lanes] * shares[g % 9]
            adv = base_ref[rows, lanes] + gain_ref[rows, lanes] * inflow
            adv_ref[rows, lanes] = adv
            freq = fc_ref[rows, :]
            term = freq * adv
            energy = energy + term
            moment = moment + freq * term
        erow = jnp.sum(energy, axis=0, keepdims=True) * _KAPPA
        mrow = jnp.sum(moment, axis=0, keepdims=True) * _KAPPA
        for r in range(8):
            sums_ref[r, pl.ds(b, 1), :] = erow
            sums_ref[r, pl.ds(b + 8, 1), :] = mrow
        return carry

    lax.fori_loop(0, 8, node_block, 0, unroll=4)


OUT_ROWS = ((0, 5), (5, 10), (10, 15), (15, 21))


def source_kernel(sums_ref, adv_ref, wind_ref, fc_ref, out_hbm, energy_ref, damp, out_ref, sem):
    spec = lax.axis_index("spec")
    total = sums_ref[0]
    for r in range(1, 8):
        total = total + sums_ref[r]
    energy = total[0:8]
    moment = total[8:16]
    mean = (moment + 4e-8) / (energy + 1e-6)
    scaled = mean / 0.8
    steep = energy * (scaled * scaled) * (scaled * scaled)
    damp[...] = (0.25 * steep) * steep / mean
    mine = lax.broadcasted_iota(jnp.int32, (8, LANES), 0) == spec
    energy_ref[...] = jnp.sum(jnp.where(mine, energy, 0.0), axis=0, keepdims=True)
    rate = [row8(damp[b : b + 1, :]) for b in range(8)]
    copies = []
    for i, (first, last) in enumerate(OUT_ROWS):
        for g in range(first, last):
            n = 8 if g < 20 else 2
            rows = slice(8 * g, 8 * g + 8)
            freq = fc_ref[rows, :]
            for b in range(8):
                lanes = slice(LANES * b, LANES * b + LANES)
                value = adv_ref[rows, lanes] * jnp.exp(wind_ref[rows, lanes] - rate[b] * freq)
                out_ref[8 * g : 8 * g + n, lanes] = value[0:n]
        rows = pl.ds(8 * first, min(8 * last, 162) - 8 * first)
        copies.append(
            pltpu.make_async_copy(out_ref.at[rows, :], out_hbm.at[rows, :], sem.at[i])
        )
        copies[i].start()
    for copy in copies:
        copy.wait()


VMEM = pl.BlockSpec(memory_space=pltpu.VMEM)
ANY = pl.BlockSpec(memory_space=pl.ANY)
F32 = jnp.float32
I32 = jnp.int32


def shape(*dims, dtype=jnp.float32):
    return jax.ShapeDtypeStruct(dims, dtype)


def cost(flops, size):
    return pl.CostEstimate(flops=flops, bytes_accessed=size, transcendentals=0)


LIMIT = pltpu.CompilerParams(vmem_limit_bytes=24 << 20)


def per_device(
    spectra,
    wet_mask,
    depth_class,
    cg_table,
    neighbour,
    edge_weight,
    edge_angle,
    send_list,
    friction,
    wind_dir,
):
    wet = wet_mask.reshape(8, LANES)
    table = jnp.asarray(_tables())
    plan = jnp.concatenate([wet, jnp.pad(send_list[0], ((0, 0), (0, LANES - GHOST)))])
    *outgoing, masked, packed = pl.pallas_call(
        send_kernel,
        out_shape=(shape(PACK, LANES),) * 5 + (shape(168, 1024), shape(PACK, 1024, dtype=I32)),
        in_specs=[ANY, VMEM],
        out_specs=(VMEM,) * 7,
        scratch_shapes=[
            pltpu.VMEM((162, 1024), F32),
            pltpu.VMEM((3, 8, LANES), I32),
            pltpu.VMEM((3, PACK, LANES), I32),
            pltpu.SemaphoreType.DMA((4,)),
        ],
        compiler_params=pltpu.CompilerParams(vmem_limit_bytes=53600 << 10),
        name="send_pack",
    )(spectra, plan)
    ghosts = [
        lax.ppermute(outgoing[k], "space", [(i, (i + o) % 32) for i in range(32)])
        for k, o in enumerate(OFFSETS)
    ]
    base, gain, wind, freq, geo, code = pl.pallas_call(
        local_kernel,
        out_shape=(
            shape(168, 1024),
            shape(168, 1024),
            shape(168, 1024),
            shape(168, LANES),
            shape(2, 8, 1024),
            shape(8, 1024, dtype=I32),
        ),
        in_specs=[VMEM] * 11,
        out_specs=(VMEM,) * 6,
        scratch_shapes=[
            pltpu.VMEM((168, LANES), F32),
            pltpu.VMEM((2, 8, 1024), F32),
            pltpu.VMEM((2, 8, LANES), F32),
        ],
        compiler_params=LIMIT,
        cost_estimate=cost(20_000_000, 4_000_000),
        name="local_slots",
    )(
        masked,
        packed,
        wet,
        neighbour,
        edge_weight,
        edge_angle,
        depth_class.reshape(8, LANES),
        cg_table,
        friction.reshape(8, LANES),
        wind_dir.reshape(8, LANES),
        table,
    )
    advected, sums = pl.pallas_call(
        ghost_kernel,
        out_shape=(shape(168, 1024), shape(8, 16, LANES)),
        in_specs=[VMEM] * 12,
        out_specs=(VMEM,) * 2,
        scratch_shapes=[pltpu.VMEM((PACK, 3 * LANES), I32)],
        compiler_params=LIMIT,
        name="ghost_slots",
    )(*ghosts, masked, base, gain, freq, geo, code, table)
    parts = lax.all_to_all(sums, "spec", split_axis=0, concat_axis=0, tiled=True)
    result, energy = pl.pallas_call(
        source_kernel,
        out_shape=(shape(162, 1024), shape(1, LANES)),
        in_specs=[VMEM] * 4,
        out_specs=(ANY, VMEM),
        scratch_shapes=[
            pltpu.VMEM((8, LANES), F32),
            pltpu.VMEM((162, 1024), F32),
            pltpu.SemaphoreType.DMA((4,)),
        ],
        compiler_params=LIMIT,
        name="source",
    )(parts, advected, wind, freq)
    return result, energy.reshape(LANES)


def solution(mesh):
    placed = (
        P("spec", "space"),
        P("space"),
        P("space"),
        P(),
        P(None, "space"),
        P(None, "space"),
        P(None, "space"),
        P("space", None, None),
        P("space"),
        P("space"),
    )
    return jax.shard_map(
        per_device,
        mesh=mesh,
        in_specs=placed,
        out_specs=(P("spec", "space"), P(("space", "spec"))),
        check_vma=False,
    )
```

```python
import math

import numpy as np
import jax
import jax.numpy as jnp
from jax import lax
from jax.experimental import pallas as pl
from jax.experimental.pallas import tpu as pltpu
from jax.sharding import PartitionSpec as P

NDIR = 36
NFREQ = 36
GHOST = 64
LANES = 128
PACK = 88
OFFSETS = (1, 31, 2, 30, 16)
SCALE = 32767.5

_F = 0.04 * np.exp(np.arange(NFREQ) * math.log(1.1))
_KAPPA = float(0.1 / (NDIR * np.sum(0.1 * _F)))
_FTOP = float(_F[-1])


def _tables():
    angle = 2.0 * np.pi * (np.arange(72) % NDIR) / NDIR
    cosine = np.repeat(np.cos(angle)[:, None], LANES, 1)
    sine = np.repeat(np.sin(angle)[:, None], LANES, 1)
    freq = np.zeros((40, LANES))
    freq[:NFREQ] = _F[:, None]
    return np.concatenate([cosine, sine, freq]).astype(np.float32)


def lane_gather(values, index):
    return jnp.take_along_axis(values, index, axis=1, mode="promise_in_bounds")


def pick(blocks, index, bits):
    level = [lane_gather(block, index) for block in blocks]
    for bit in bits:
        level = [
            jnp.where(bit, level[i + 1], level[i]) if i + 1 < len(level) else level[i]
            for i in range(0, len(level), 2)
        ]
    return level[0]


def row8(row):
    return jnp.broadcast_to(row, (8, LANES))


def turn(angle):
    h = 0.5 * angle
    t = h * h
    s = h * (
        1.0
        + t
        * (
            -1.6666666666e-1
            + t * (8.3333331e-3 + t * (-1.98412e-4 + t * (2.75567e-6 - t * 2.4700e-8)))
        )
    )
    c = 1.0 + t * (
        -0.5
        + t * (4.16666664e-2 + t * (-1.3888883e-3 + t * (2.480065e-5 + t * (-2.75358e-7 + t * 2.065e-9))))
    )
    return 1.0 - 2.0 * s * s, 2.0 * s * c


MATRIX_SLOTS = 4
GHOST_SLOTS = 3
HALF = 176
GHOST_HALF = 192
CHUNKS = ((0, 6), (6, 11))


def send_kernel(
    x_hbm, plan_ref, o0, o1, o2, o3, o4, masked_ref, packed_ref, x_ref, code_ref,
    words_ref, sem
):
    outs = (o0, o1, o2, o3, o4)
    copies = []
    for i, (first, last) in enumerate(CHUNKS):
        for j, base in enumerate((0, PACK)):
            rows = pl.ds(base + 8 * first, min(8 * last + base, 162) - base - 8 * first)
            copies.append(
                pltpu.make_async_copy(x_hbm.at[rows, :], x_ref.at[rows, :], sem.at[2 * i + j])
            )
    for copy in copies:
        copy.start()
    me = lax.axis_index("space")
    lane = lax.broadcasted_iota(jnp.int32, (8, LANES), 1)
    low = lane < GHOST
    rows = [plan_ref[pl.ds(8 + ((me + o) & 31), 1), 0:GHOST] for o in OFFSETS]
    for q, (a, b) in enumerate(((0, 1), (2, 3), (4, 4))):
        code_ref[q] = row8(jnp.concatenate([rows[a], rows[b]], axis=1))
    wet = [row8(plan_ref[b : b + 1, :].astype(jnp.float32)) for b in range(8)]

    def load(g, b):
        lanes = slice(LANES * b, LANES * b + LANES)
        if g < 20:
            value = x_ref[8 * g : 8 * g + 8, lanes] * wet[b]
        else:
            zero = jnp.zeros((6, LANES), jnp.float32)
            value = jnp.concatenate([x_ref[160:162, lanes], zero], axis=0) * wet[b]
        masked_ref[8 * g : 8 * g + 8, lanes] = value
        return (value * SCALE + 0.5).astype(jnp.int32)

    for i, (first, last) in enumerate(CHUNKS):
        copies[2 * i].wait()
        copies[2 * i + 1].wait()
        for g in range(first, last):
            for b in range(8):
                word = load(g, b) << 16
                if g < 10:
                    word = word | load(g + 11, b)
                packed_ref[8 * g : 8 * g + 8, LANES * b : LANES * b + LANES] = word

    def gather(q, carry):
        full = code_ref[q]
        index = full & 127
        bits = [(full & (128 << i)) != 0 for i in range(3)]
        for g in range(11):
            rows = slice(8 * g, 8 * g + 8)
            words_ref[q, rows, :] = pick(
                [packed_ref[rows, LANES * b : LANES * b + LANES] for b in range(8)], index, bits
            )
        return carry

    lax.fori_loop(0, 3, gather, 0)
    for q in range(3):
        for g in range(11):
            rows = slice(8 * g, 8 * g + 8)
            word = words_ref[q, rows, :]
            top = lax.shift_right_logical(word, 16).astype(jnp.float32)
            bottom = (word & 65535).astype(jnp.float32)
            if q < 2:
                outs[2 * q][rows, :] = jnp.where(low, top, pltpu.roll(bottom, 64, 1))
                outs[2 * q + 1][rows, :] = jnp.where(low, pltpu.roll(top, 64, 1), bottom)
            else:
                outs[4][rows, :] = jnp.where(low, top, bottom)


def slots(packed, blocks, code, geo, tab_ref, lanes, bit_count, product, columns, ready):
    total = [None] * 21
    shares = [None] * 9
    for m in list(range(ready, 8)) + list(range(ready)):
        full = row8(code[m : m + 1, lanes])
        index = full & 127
        bits = [(full & (128 << i)) != 0 for i in range(bit_count)]
        wc = row8(geo[0, m : m + 1, lanes])
        ws = row8(geo[1, m : m + 1, lanes])
        share = [
            jnp.maximum(
                tab_ref[8 * r : 8 * r + 8, :] * wc + tab_ref[72 + 8 * r : 80 + 8 * r, :] * ws, 0.0
            )
            for r in range(9)
        ]
        shares = [s if t is None else t + s for t, s in zip(shares, share)]
        if m < ready:
            for h in range(21):
                half = product.shape[1] // 2
                row = 8 * h + (8 if half > HALF and h > 10 else 0)
                high = product[m, row : row + 8, columns]
                low = product[m, half + row : half + row + 8, columns]
                term = share[h % 9] * (high + low)
                total[h] = term if total[h] is None else total[h] + term
            continue
        for g in range(11):
            word = pick(
                [packed[8 * g : 8 * g + 8, LANES * s : LANES * s + LANES] for s in range(blocks)],
                index,
                bits,
            )
            for h, value in ((g, lax.shift_right_logical(word, 16)), (g + 11, word & 65535)):
                if h < 21:
                    term = share[h % 9] * value.astype(jnp.float32)
                    total[h] = term if total[h] is None else total[h] + term
    return total, shares


def split(value):
    high = value.astype(jnp.bfloat16)
    return high, (value - high.astype(jnp.float32)).astype(jnp.bfloat16)


def matrix_slots(count, code, pair, blocks, count_ref, hot_ref, parts_ref, product_ref):
    size = count_ref.shape[0]
    for m in range(count):
        entry = code[m : m + 1, pair]
        for j in range(blocks):
            wanted = (entry - size * j).astype(jnp.float32).astype(jnp.bfloat16)
            hit = count_ref[...] == jnp.broadcast_to(wanted, (size, 256))
            hot_ref[m, size * j : size * j + size, :] = jnp.where(
                hit, jnp.bfloat16(1), jnp.bfloat16(0)
            )
        product_ref[m] = jnp.dot(parts_ref[...], hot_ref[m], preferred_element_type=jnp.float32)


def local_kernel(
    x_ref,
    packed,
    wet_ref,
    nb_ref,
    ew_ref,
    ea_ref,
    dc_ref,
    cg_ref,
    fr_ref,
    wd_ref,
    tab_ref,
    base_ref,
    gain_ref,
    wind_ref,
    fc_ref,
    geo_ref,
    code_ref,
    cgx,
    wloc,
    drive_ref,
    parts_ref,
    count_ref,
    hot_ref,
    product_ref,
):
    me = lax.axis_index("space")
    spec = lax.axis_index("spec")
    par = spec & 1
    first_freq = (9 * spec) >> 1
    sign = (1 - 2 * par).astype(jnp.float32)
    entry = nb_ref[...]
    ghost = entry >= 1024
    weight = ew_ref[...] * sign
    cosine, sine = turn(ea_ref[...])
    wc = weight * cosine
    ws = weight * sine
    wloc[0] = jnp.where(ghost, 0.0, wc)
    wloc[1] = jnp.where(ghost, 0.0, ws)
    geo_ref[0] = jnp.where(ghost, wc, 0.0)
    geo_ref[1] = jnp.where(ghost, ws, 0.0)
    peer = (entry - 1024) >> 6
    off = (me - peer) & 31
    half = (off == 31) | (off == 30)
    block = jnp.where(off == 16, 2, jnp.where((off == 2) | (off == 30), 1, 0))
    code_ref[...] = (entry & 63) + jnp.where(half, 64, 0) + 128 * block
    drive4 = fr_ref[...] * (sign * 4.0 / _FTOP)
    cosine, sine = turn(wd_ref[...])
    drive_ref[0] = drive4 * cosine
    drive_ref[1] = drive4 * sine
    cgpad = [None] * 5
    fpad = [None] * 5
    for j in range(5):
        line = cg_ref[pl.ds(first_freq + j, 1), :]
        cgpad[j] = row8(jnp.concatenate([line, line, line, line], axis=1))
        fpad[j] = row8(tab_ref[pl.ds(144 + first_freq + j, 1), :])
    for g in range(21):
        comp = lax.broadcasted_iota(jnp.int32, (8, LANES), 0) + 8 * g + 18 * par
        cv, fv = cgpad[0], fpad[0]
        for j in range(1, 5):
            if 8 * g + 7 + 18 >= 36 * j:
                later = comp >= 36 * j
                cv = jnp.where(later, cgpad[j], cv)
                fv = jnp.where(later, fpad[j], fv)
        cgx[8 * g : 8 * g + 8, :] = cv
        fc_ref[8 * g : 8 * g + 8, :] = fv

    for g in range(11):
        rows = slice(16 * g, 16 * g + 16)
        for b in range(8):
            lanes = slice(LANES * b, LANES * b + LANES)
            if g < 10:
                value = x_ref[rows, lanes] * SCALE
            else:
                value = jnp.concatenate(
                    [x_ref[160:168, lanes] * SCALE, jnp.zeros((8, LANES), jnp.float32)], axis=0
                )
            parts_ref[rows, lanes], parts_ref[HALF + 16 * g : HALF + 16 * g + 16, lanes] = split(
                value
            )
    count_ref[...] = lax.broadcasted_iota(jnp.int32, (256, 256), 0).astype(jnp.bfloat16)

    def node_pair(p, carry):
        pair = pl.ds(pl.multiple_of(p * 256, 256), 256)
        matrix_slots(MATRIX_SLOTS, nb_ref, pair, 4, count_ref, hot_ref, parts_ref, product_ref)
        for k in range(2):
            node_block(2 * p + k, slice(LANES * k, LANES * k + LANES))
        return carry

    def node_block(b, columns):
        lanes = pl.ds(pl.multiple_of(b * LANES, LANES), LANES)
        wet = row8(wet_ref[pl.ds(b, 1), :].astype(jnp.float32))
        cls = row8(dc_ref[pl.ds(b, 1), :])
        total, shares = slots(
            packed, 8, nb_ref, wloc, tab_ref, lanes, 3, product_ref, columns, MATRIX_SLOTS
        )
        dcos = row8(drive_ref[0, pl.ds(b, 1), :])
        dsin = row8(drive_ref[1, pl.ds(b, 1), :])
        for g in range(21):
            rows = slice(8 * g, 8 * g + 8)
            gain = wet * lane_gather(cgx[rows, :], cls)
            gain_ref[rows, lanes] = gain
            x = x_ref[rows, lanes]
            base_ref[rows, lanes] = x + gain * (total[g] * (1.0 / SCALE) - x * shares[g % 9])
            r = 8 * (g % 9)
            drive = tab_ref[r : r + 8, :] * dcos + tab_ref[72 + r : 80 + r, :] * dsin
            wind_ref[rows, lanes] = 0.125 * jnp.maximum(fc_ref[rows, :] * drive - 1.0, 0.0)

    lax.fori_loop(0, 4, node_pair, 0, unroll=2)


def ghost_kernel(
    g0, g1, g2, g3, g4, x_ref, base_ref, gain_ref, fc_ref, geo_ref, code_ref, tab_ref, adv_ref,
    sums_ref, packed, parts_ref, count_ref, hot_ref, product_ref
):
    low = lax.broadcasted_iota(jnp.int32, (8, LANES), 1) < GHOST
    for g in range(11):
        rows = slice(8 * g, 8 * g + 8)
        whole = [ref[rows, :].astype(jnp.int32) for ref in (g0, g1, g2, g3, g4)]
        for q in range(3):
            a = whole[2 * q]
            word = (a << 16) | pltpu.roll(a, 64, 1)
            if q < 2:
                c = whole[2 * q + 1]
                word = jnp.where(low, word, (pltpu.roll(c, 64, 1) << 16) | c)
            packed[rows, LANES * q : LANES * q + LANES] = word

    zero = jnp.zeros((8, 3 * LANES), jnp.float32)
    for h in range(2):
        for g in range(0, 11, 2):
            word = packed[8 * g : min(8 * g + 16, PACK), :]
            value = (word & 65535) if h else lax.shift_right_logical(word, 16)
            value = value.astype(jnp.float32)
            if g == 10:
                value = jnp.concatenate([value, zero], axis=0)
            first = 96 * h + 8 * g
            parts_ref[first : first + 16, :], parts_ref[
                GHOST_HALF + first : GHOST_HALF + first + 16, :
            ] = split(value)
    count_ref[...] = lax.broadcasted_iota(jnp.int32, (LANES, 256), 0).astype(jnp.bfloat16)

    def node_pair(p, carry):
        pair = pl.ds(pl.multiple_of(p * 256, 256), 256)
        matrix_slots(GHOST_SLOTS, code_ref, pair, 3, count_ref, hot_ref, parts_ref, product_ref)
        for k in range(2):
            node_block(2 * p + k, slice(LANES * k, LANES * k + LANES))
        return carry

    def node_block(b, columns):
        lanes = pl.ds(pl.multiple_of(b * LANES, LANES), LANES)
        total, shares = slots(
            packed, 3, code_ref, geo_ref, tab_ref, lanes, 2, product_ref, columns, GHOST_SLOTS
        )
        energy = jnp.zeros((8, LANES), jnp.float32)
        moment = jnp.zeros((8, LANES), jnp.float32)
        for g in range(21):
            rows = slice(8 * g, 8 * g + 8)
            inflow = total[g] * (1.0 / SCALE) - x_ref[rows, lanes] * shares[g % 9]
            adv = base_ref[rows, lanes] + gain_ref[rows, lanes] * inflow
            adv_ref[rows, lanes] = adv
            freq = fc_ref[rows, :]
            term = freq * adv
            energy = energy + term
            moment = moment + freq * term
        erow = jnp.sum(energy, axis=0, keepdims=True) * _KAPPA
        mrow = jnp.sum(moment, axis=0, keepdims=True) * _KAPPA
        for r in range(8):
            sums_ref[r, pl.ds(b, 1), :] = erow
            sums_ref[r, pl.ds(b + 8, 1), :] = mrow

    lax.fori_loop(0, 4, node_pair, 0, unroll=2)


OUT_ROWS = ((0, 5), (5, 10), (10, 15), (15, 21))


def source_kernel(sums_ref, adv_ref, wind_ref, fc_ref, out_hbm, energy_ref, damp, out_ref, sem):
    spec = lax.axis_index("spec")
    total = sums_ref[0]
    for r in range(1, 8):
        total = total + sums_ref[r]
    energy = total[0:8]
    moment = total[8:16]
    mean = (moment + 4e-8) / (energy + 1e-6)
    scaled = mean / 0.8
    steep = energy * (scaled * scaled) * (scaled * scaled)
    damp[...] = (0.25 * steep) * steep / mean
    mine = lax.broadcasted_iota(jnp.int32, (8, LANES), 0) == spec
    energy_ref[...] = jnp.sum(jnp.where(mine, energy, 0.0), axis=0, keepdims=True)
    rate = [row8(damp[b : b + 1, :]) for b in range(8)]
    copies = []
    for i, (first, last) in enumerate(OUT_ROWS):
        for g in range(first, last):
            n = 8 if g < 20 else 2
            rows = slice(8 * g, 8 * g + 8)
            freq = fc_ref[rows, :]
            for b in range(8):
                lanes = slice(LANES * b, LANES * b + LANES)
                value = adv_ref[rows, lanes] * jnp.exp(wind_ref[rows, lanes] - rate[b] * freq)
                out_ref[8 * g : 8 * g + n, lanes] = value[0:n]
        rows = pl.ds(8 * first, min(8 * last, 162) - 8 * first)
        copies.append(
            pltpu.make_async_copy(out_ref.at[rows, :], out_hbm.at[rows, :], sem.at[i])
        )
        copies[i].start()
    for copy in copies:
        copy.wait()


VMEM = pl.BlockSpec(memory_space=pltpu.VMEM)
ANY = pl.BlockSpec(memory_space=pl.ANY)
F32 = jnp.float32
I32 = jnp.int32


def shape(*dims, dtype=jnp.float32):
    return jax.ShapeDtypeStruct(dims, dtype)


def cost(flops, size):
    return pl.CostEstimate(flops=flops, bytes_accessed=size, transcendentals=0)


LIMIT = pltpu.CompilerParams(vmem_limit_bytes=24 << 20)


def per_device(
    spectra,
    wet_mask,
    depth_class,
    cg_table,
    neighbour,
    edge_weight,
    edge_angle,
    send_list,
    friction,
    wind_dir,
):
    wet = wet_mask.reshape(8, LANES)
    table = jnp.asarray(_tables())
    plan = jnp.concatenate([wet, jnp.pad(send_list[0], ((0, 0), (0, LANES - GHOST)))])
    *outgoing, masked, packed = pl.pallas_call(
        send_kernel,
        out_shape=(shape(PACK, LANES),) * 5 + (shape(168, 1024), shape(PACK, 1024, dtype=I32)),
        in_specs=[ANY, VMEM],
        out_specs=(VMEM,) * 7,
        scratch_shapes=[
            pltpu.VMEM((162, 1024), F32),
            pltpu.VMEM((3, 8, LANES), I32),
            pltpu.VMEM((3, PACK, LANES), I32),
            pltpu.SemaphoreType.DMA((4,)),
        ],
        compiler_params=pltpu.CompilerParams(vmem_limit_bytes=53600 << 10),
        name="send_pack",
    )(spectra, plan)
    ghosts = [
        lax.ppermute(outgoing[k], "space", [(i, (i + o) % 32) for i in range(32)])
        for k, o in enumerate(OFFSETS)
    ]
    base, gain, wind, freq, geo, code = pl.pallas_call(
        local_kernel,
        out_shape=(
            shape(168, 1024),
            shape(168, 1024),
            shape(168, 1024),
            shape(168, LANES),
            shape(2, 8, 1024),
            shape(8, 1024, dtype=I32),
        ),
        in_specs=[VMEM] * 11,
        out_specs=(VMEM,) * 6,
        scratch_shapes=[
            pltpu.VMEM((168, LANES), F32),
            pltpu.VMEM((2, 8, 1024), F32),
            pltpu.VMEM((2, 8, LANES), F32),
            pltpu.VMEM((2 * HALF, 1024), jnp.bfloat16),
            pltpu.VMEM((256, 256), jnp.bfloat16),
            pltpu.VMEM((MATRIX_SLOTS, 1024, 256), jnp.bfloat16),
            pltpu.VMEM((MATRIX_SLOTS, 2 * HALF, 256), F32),
        ],
        compiler_params=LIMIT,
        cost_estimate=cost(20_000_000, 4_000_000),
        name="local_slots",
    )(
        masked,
        packed,
        wet,
        neighbour,
        edge_weight,
        edge_angle,
        depth_class.reshape(8, LANES),
        cg_table,
        friction.reshape(8, LANES),
        wind_dir.reshape(8, LANES),
        table,
    )
    advected, sums = pl.pallas_call(
        ghost_kernel,
        out_shape=(shape(168, 1024), shape(8, 16, LANES)),
        in_specs=[VMEM] * 12,
        out_specs=(VMEM,) * 2,
        scratch_shapes=[
            pltpu.VMEM((PACK, 3 * LANES), I32),
            pltpu.VMEM((2 * GHOST_HALF, 3 * LANES), jnp.bfloat16),
            pltpu.VMEM((LANES, 256), jnp.bfloat16),
            pltpu.VMEM((GHOST_SLOTS, 3 * LANES, 256), jnp.bfloat16),
            pltpu.VMEM((GHOST_SLOTS, 2 * GHOST_HALF, 256), F32),
        ],
        compiler_params=LIMIT,
        name="ghost_slots",
    )(*ghosts, masked, base, gain, freq, geo, code, table)
    parts = lax.all_to_all(sums, "spec", split_axis=0, concat_axis=0, tiled=True)
    result, energy = pl.pallas_call(
        source_kernel,
        out_shape=(shape(162, 1024), shape(1, LANES)),
        in_specs=[VMEM] * 4,
        out_specs=(ANY, VMEM),
        scratch_shapes=[
            pltpu.VMEM((8, LANES), F32),
            pltpu.VMEM((162, 1024), F32),
            pltpu.SemaphoreType.DMA((4,)),
        ],
        compiler_params=LIMIT,
        name="source",
    )(parts, advected, wind, freq)
    return result, energy.reshape(LANES)


def solution(mesh):
    placed = (
        P("spec", "space"),
        P("space"),
        P("space"),
        P(),
        P(None, "space"),
        P(None, "space"),
        P(None, "space"),
        P("space", None, None),
        P("space"),
        P("space"),
    )
    return jax.shard_map(
        per_device,
        mesh=mesh,
        in_specs=placed,
        out_specs=(P("spec", "space"), P(("space", "spec"))),
        check_vma=False,
    )
```

```python
import math

import numpy as np
import jax
import jax.numpy as jnp
from jax import lax
from jax.experimental import pallas as pl
from jax.experimental.pallas import tpu as pltpu
from jax.sharding import PartitionSpec as P

NDIR = 36
NFREQ = 36
GHOST = 64
LANES = 128
PACK = 88
OFFSETS = (1, 31, 2, 30, 16)
SCALE = 32767.5

_F = 0.04 * np.exp(np.arange(NFREQ) * math.log(1.1))
_KAPPA = float(0.1 / (NDIR * np.sum(0.1 * _F)))
_FTOP = float(_F[-1])


def _tables():
    angle = 2.0 * np.pi * (np.arange(72) % NDIR) / NDIR
    cosine = np.repeat(np.cos(angle)[:, None], LANES, 1)
    sine = np.repeat(np.sin(angle)[:, None], LANES, 1)
    freq = np.zeros((40, LANES))
    freq[:NFREQ] = _F[:, None]
    return np.concatenate([cosine, sine, freq]).astype(np.float32)


def lane_gather(values, index):
    return jnp.take_along_axis(values, index, axis=1, mode="promise_in_bounds")


def pick(blocks, index, bits):
    level = [lane_gather(block, index) for block in blocks]
    for bit in bits:
        level = [
            jnp.where(bit, level[i + 1], level[i]) if i + 1 < len(level) else level[i]
            for i in range(0, len(level), 2)
        ]
    return level[0]


def row8(row):
    return jnp.broadcast_to(row, (8, LANES))


def turn(angle):
    h = 0.5 * angle
    t = h * h
    s = h * (
        1.0
        + t
        * (
            -1.6666666666e-1
            + t * (8.3333331e-3 + t * (-1.98412e-4 + t * (2.75567e-6 - t * 2.4700e-8)))
        )
    )
    c = 1.0 + t * (
        -0.5
        + t * (4.16666664e-2 + t * (-1.3888883e-3 + t * (2.480065e-5 + t * (-2.75358e-7 + t * 2.065e-9))))
    )
    return 1.0 - 2.0 * s * s, 2.0 * s * c


MATRIX_SLOTS = 4
GHOST_SLOTS = 3
HALF = 176
GHOST_HALF = 192
CHUNKS = ((0, 6), (6, 11))


def send_kernel(
    x_hbm, plan_ref, o0, o1, o2, o3, o4, masked_ref, packed_ref, x_ref, code_ref,
    words_ref, sem
):
    outs = (o0, o1, o2, o3, o4)
    copies = []
    for i, (first, last) in enumerate(CHUNKS):
        for j, base in enumerate((0, PACK)):
            rows = pl.ds(base + 8 * first, min(8 * last + base, 162) - base - 8 * first)
            copies.append(
                pltpu.make_async_copy(x_hbm.at[rows, :], x_ref.at[rows, :], sem.at[2 * i + j])
            )
    for copy in copies:
        copy.start()
    me = lax.axis_index("space")
    lane = lax.broadcasted_iota(jnp.int32, (8, LANES), 1)
    low = lane < GHOST
    rows = [plan_ref[pl.ds(8 + ((me + o) & 31), 1), 0:GHOST] for o in OFFSETS]
    for q, (a, b) in enumerate(((0, 1), (2, 3), (4, 4))):
        code_ref[q] = row8(jnp.concatenate([rows[a], rows[b]], axis=1))
    wet = [row8(plan_ref[b : b + 1, :].astype(jnp.float32)) for b in range(8)]

    def load(g, b):
        lanes = slice(LANES * b, LANES * b + LANES)
        if g < 20:
            value = x_ref[8 * g : 8 * g + 8, lanes] * wet[b]
        else:
            zero = jnp.zeros((6, LANES), jnp.float32)
            value = jnp.concatenate([x_ref[160:162, lanes], zero], axis=0) * wet[b]
        masked_ref[8 * g : 8 * g + 8, lanes] = value
        return (value * SCALE + 0.5).astype(jnp.int32)

    for i, (first, last) in enumerate(CHUNKS):
        copies[2 * i].wait()
        copies[2 * i + 1].wait()
        for g in range(first, last):
            for b in range(8):
                word = load(g, b) << 16
                if g < 10:
                    word = word | load(g + 11, b)
                packed_ref[8 * g : 8 * g + 8, LANES * b : LANES * b + LANES] = word

    def gather(q, carry):
        full = code_ref[q]
        index = full & 127
        bits = [(full & (128 << i)) != 0 for i in range(3)]
        for g in range(11):
            rows = slice(8 * g, 8 * g + 8)
            words_ref[q, rows, :] = pick(
                [packed_ref[rows, LANES * b : LANES * b + LANES] for b in range(8)], index, bits
            )
        return carry

    lax.fori_loop(0, 3, gather, 0)
    for q in range(3):
        for g in range(11):
            rows = slice(8 * g, 8 * g + 8)
            word = words_ref[q, rows, :]
            top = lax.shift_right_logical(word, 16).astype(jnp.float32)
            bottom = (word & 65535).astype(jnp.float32)
            if q < 2:
                outs[2 * q][rows, :] = jnp.where(low, top, pltpu.roll(bottom, 64, 1))
                outs[2 * q + 1][rows, :] = jnp.where(low, pltpu.roll(top, 64, 1), bottom)
            else:
                outs[4][rows, :] = jnp.where(low, top, bottom)


def slots(packed, blocks, code, geo, tab_ref, lanes, bit_count, product, columns, ready):
    total = [None] * 21
    shares = [None] * 9
    for m in list(range(ready, 8)) + list(range(ready)):
        full = row8(code[m : m + 1, lanes])
        index = full & 127
        bits = [(full & (128 << i)) != 0 for i in range(bit_count)]
        wc = row8(geo[0, m : m + 1, lanes])
        ws = row8(geo[1, m : m + 1, lanes])
        share = [
            jnp.maximum(
                tab_ref[8 * r : 8 * r + 8, :] * wc + tab_ref[72 + 8 * r : 80 + 8 * r, :] * ws, 0.0
            )
            for r in range(9)
        ]
        shares = [s if t is None else t + s for t, s in zip(shares, share)]
        if m < ready:
            for h in range(21):
                half = product.shape[1] // 2
                row = 8 * h + (8 if half > HALF and h > 10 else 0)
                high = product[m, row : row + 8, columns]
                low = product[m, half + row : half + row + 8, columns]
                term = share[h % 9] * (high + low)
                total[h] = term if total[h] is None else total[h] + term
            continue
        for g in range(11):
            word = pick(
                [packed[8 * g : 8 * g + 8, LANES * s : LANES * s + LANES] for s in range(blocks)],
                index,
                bits,
            )
            for h, value in ((g, lax.shift_right_logical(word, 16)), (g + 11, word & 65535)):
                if h < 21:
                    term = share[h % 9] * value.astype(jnp.float32)
                    total[h] = term if total[h] is None else total[h] + term
    return total, shares


def split(value):
    high = value.astype(jnp.bfloat16)
    return high, (value - high.astype(jnp.float32)).astype(jnp.bfloat16)


def matrix_slots(count, code, pair, blocks, count_ref, hot_ref, parts_ref, product_ref):
    size = count_ref.shape[0]
    for m in range(count):
        entry = code[m : m + 1, pair]
        for j in range(blocks):
            wanted = (entry - size * j).astype(jnp.float32).astype(jnp.bfloat16)
            hit = count_ref[...] == jnp.broadcast_to(wanted, (size, 256))
            hot_ref[m, size * j : size * j + size, :] = jnp.where(
                hit, jnp.bfloat16(1), jnp.bfloat16(0)
            )
        product_ref[m] = jnp.dot(parts_ref[...], hot_ref[m], preferred_element_type=jnp.float32)


def local_kernel(
    x_ref,
    packed,
    wet_ref,
    nb_ref,
    ew_ref,
    ea_ref,
    dc_ref,
    cg_ref,
    fr_ref,
    wd_ref,
    tab_ref,
    base_ref,
    gain_ref,
    wind_ref,
    fc_ref,
    geo_ref,
    code_ref,
    cgx,
    wloc,
    drive_ref,
    parts_ref,
    count_ref,
    hot_ref,
    product_ref,
):
    me = lax.axis_index("space")
    spec = lax.axis_index("spec")
    par = spec & 1
    first_freq = (9 * spec) >> 1
    sign = (1 - 2 * par).astype(jnp.float32)
    entry = nb_ref[...]
    ghost = entry >= 1024
    weight = ew_ref[...] * sign
    cosine, sine = turn(ea_ref[...])
    wc = weight * cosine
    ws = weight * sine
    wloc[0] = jnp.where(ghost, 0.0, wc)
    wloc[1] = jnp.where(ghost, 0.0, ws)
    geo_ref[0] = jnp.where(ghost, wc, 0.0)
    geo_ref[1] = jnp.where(ghost, ws, 0.0)
    peer = (entry - 1024) >> 6
    off = (me - peer) & 31
    half = (off == 31) | (off == 30)
    block = jnp.where(off == 16, 2, jnp.where((off == 2) | (off == 30), 1, 0))
    code_ref[...] = (entry & 63) + jnp.where(half, 64, 0) + 128 * block
    drive4 = fr_ref[...] * (sign * 4.0 / _FTOP)
    cosine, sine = turn(wd_ref[...])
    drive_ref[0] = drive4 * cosine
    drive_ref[1] = drive4 * sine
    cgpad = [None] * 5
    fpad = [None] * 5
    for j in range(5):
        line = cg_ref[pl.ds(first_freq + j, 1), :]
        cgpad[j] = row8(jnp.concatenate([line, line, line, line], axis=1))
        fpad[j] = row8(tab_ref[pl.ds(144 + first_freq + j, 1), :])
    for g in range(21):
        comp = lax.broadcasted_iota(jnp.int32, (8, LANES), 0) + 8 * g + 18 * par
        cv, fv = cgpad[0], fpad[0]
        for j in range(1, 5):
            if 8 * g + 7 + 18 >= 36 * j:
                later = comp >= 36 * j
                cv = jnp.where(later, cgpad[j], cv)
                fv = jnp.where(later, fpad[j], fv)
        cgx[8 * g : 8 * g + 8, :] = cv
        fc_ref[8 * g : 8 * g + 8, :] = fv

    for g in range(11):
        rows = slice(16 * g, 16 * g + 16)
        for b in range(8):
            lanes = slice(LANES * b, LANES * b + LANES)
            if g < 10:
                value = x_ref[rows, lanes] * SCALE
            else:
                value = jnp.concatenate(
                    [x_ref[160:168, lanes] * SCALE, jnp.zeros((8, LANES), jnp.float32)], axis=0
                )
            parts_ref[rows, lanes], parts_ref[HALF + 16 * g : HALF + 16 * g + 16, lanes] = split(
                value
            )
    count_ref[...] = lax.broadcasted_iota(jnp.int32, (256, 256), 0).astype(jnp.bfloat16)

    def node_pair(p, carry):
        pair = pl.ds(pl.multiple_of(p * 256, 256), 256)
        matrix_slots(MATRIX_SLOTS, nb_ref, pair, 4, count_ref, hot_ref, parts_ref, product_ref)
        for k in range(2):
            node_block(2 * p + k, slice(LANES * k, LANES * k + LANES))
        return carry

    def node_block(b, columns):
        lanes = pl.ds(pl.multiple_of(b * LANES, LANES), LANES)
        wet = row8(wet_ref[pl.ds(b, 1), :].astype(jnp.float32))
        cls = row8(dc_ref[pl.ds(b, 1), :])
        total, shares = slots(
            packed, 8, nb_ref, wloc, tab_ref, lanes, 3, product_ref, columns, MATRIX_SLOTS
        )
        dcos = row8(drive_ref[0, pl.ds(b, 1), :])
        dsin = row8(drive_ref[1, pl.ds(b, 1), :])
        for g in range(21):
            rows = slice(8 * g, 8 * g + 8)
            gain = wet * lane_gather(cgx[rows, :], cls)
            gain_ref[rows, lanes] = gain
            x = x_ref[rows, lanes]
            base_ref[rows, lanes] = x + gain * (total[g] * (1.0 / SCALE) - x * shares[g % 9])
            r = 8 * (g % 9)
            drive = tab_ref[r : r + 8, :] * dcos + tab_ref[72 + r : 80 + r, :] * dsin
            wind_ref[rows, lanes] = 0.125 * jnp.maximum(fc_ref[rows, :] * drive - 1.0, 0.0)

    lax.fori_loop(0, 4, node_pair, 0, unroll=2)


def ghost_kernel(
    g0, g1, g2, g3, g4, x_ref, base_ref, gain_ref, fc_ref, geo_ref, code_ref, tab_ref, adv_ref,
    sums_ref, packed, parts_ref, count_ref, hot_ref, product_ref
):
    low = lax.broadcasted_iota(jnp.int32, (8, LANES), 1) < GHOST
    for g in range(11):
        rows = slice(8 * g, 8 * g + 8)
        whole = [ref[rows, :].astype(jnp.int32) for ref in (g0, g1, g2, g3, g4)]
        for q in range(3):
            a = whole[2 * q]
            word = (a << 16) | pltpu.roll(a, 64, 1)
            if q < 2:
                c = whole[2 * q + 1]
                word = jnp.where(low, word, (pltpu.roll(c, 64, 1) << 16) | c)
            packed[rows, LANES * q : LANES * q + LANES] = word

    zero = jnp.zeros((8, 3 * LANES), jnp.float32)
    for h in range(2):
        for g in range(0, 11, 2):
            word = packed[8 * g : min(8 * g + 16, PACK), :]
            value = (word & 65535) if h else lax.shift_right_logical(word, 16)
            value = value.astype(jnp.float32)
            if g == 10:
                value = jnp.concatenate([value, zero], axis=0)
            first = 96 * h + 8 * g
            parts_ref[first : first + 16, :], parts_ref[
                GHOST_HALF + first : GHOST_HALF + first + 16, :
            ] = split(value)
    count_ref[...] = lax.broadcasted_iota(jnp.int32, (LANES, 256), 0).astype(jnp.bfloat16)

    for p in range(4):
        matrix_slots(
            GHOST_SLOTS,
            code_ref,
            slice(256 * p, 256 * p + 256),
            3,
            count_ref,
            hot_ref.at[p % 2],
            parts_ref,
            product_ref.at[p % 2],
        )
        for k in range(2):
            b = 2 * p + k
            columns = slice(LANES * k, LANES * k + LANES)
            lanes = slice(LANES * b, LANES * b + LANES)
            total, shares = slots(
                packed,
                3,
                code_ref,
                geo_ref,
                tab_ref,
                lanes,
                2,
                product_ref.at[p % 2],
                columns,
                GHOST_SLOTS,
            )
            energy = jnp.zeros((8, LANES), jnp.float32)
            moment = jnp.zeros((8, LANES), jnp.float32)
            for g in range(21):
                rows = slice(8 * g, 8 * g + 8)
                inflow = total[g] * (1.0 / SCALE) - x_ref[rows, lanes] * shares[g % 9]
                adv = base_ref[rows, lanes] + gain_ref[rows, lanes] * inflow
                adv_ref[rows, lanes] = adv
                freq = fc_ref[rows, :]
                term = freq * adv
                energy = energy + term
                moment = moment + freq * term
            erow = jnp.sum(energy, axis=0, keepdims=True) * _KAPPA
            mrow = jnp.sum(moment, axis=0, keepdims=True) * _KAPPA
            for r in range(8):
                sums_ref[r, b : b + 1, :] = erow
                sums_ref[r, b + 8 : b + 9, :] = mrow


OUT_ROWS = ((0, 5), (5, 10), (10, 15), (15, 21))


def source_kernel(sums_ref, adv_ref, wind_ref, fc_ref, out_hbm, energy_ref, damp, out_ref, sem):
    spec = lax.axis_index("spec")
    total = sums_ref[0]
    for r in range(1, 8):
        total = total + sums_ref[r]
    energy = total[0:8]
    moment = total[8:16]
    mean = (moment + 4e-8) / (energy + 1e-6)
    scaled = mean / 0.8
    steep = energy * (scaled * scaled) * (scaled * scaled)
    damp[...] = (0.25 * steep) * steep / mean
    mine = lax.broadcasted_iota(jnp.int32, (8, LANES), 0) == spec
    energy_ref[...] = jnp.sum(jnp.where(mine, energy, 0.0), axis=0, keepdims=True)
    rate = [row8(damp[b : b + 1, :]) for b in range(8)]
    copies = []
    for i, (first, last) in enumerate(OUT_ROWS):
        for g in range(first, last):
            n = 8 if g < 20 else 2
            rows = slice(8 * g, 8 * g + 8)
            freq = fc_ref[rows, :]
            for b in range(8):
                lanes = slice(LANES * b, LANES * b + LANES)
                value = adv_ref[rows, lanes] * jnp.exp(wind_ref[rows, lanes] - rate[b] * freq)
                out_ref[8 * g : 8 * g + n, lanes] = value[0:n]
        rows = pl.ds(8 * first, min(8 * last, 162) - 8 * first)
        copies.append(
            pltpu.make_async_copy(out_ref.at[rows, :], out_hbm.at[rows, :], sem.at[i])
        )
        copies[i].start()
    for copy in copies:
        copy.wait()


VMEM = pl.BlockSpec(memory_space=pltpu.VMEM)
ANY = pl.BlockSpec(memory_space=pl.ANY)
F32 = jnp.float32
I32 = jnp.int32


def shape(*dims, dtype=jnp.float32):
    return jax.ShapeDtypeStruct(dims, dtype)


def cost(flops, size):
    return pl.CostEstimate(flops=flops, bytes_accessed=size, transcendentals=0)


LIMIT = pltpu.CompilerParams(vmem_limit_bytes=24 << 20)


def per_device(
    spectra,
    wet_mask,
    depth_class,
    cg_table,
    neighbour,
    edge_weight,
    edge_angle,
    send_list,
    friction,
    wind_dir,
):
    wet = wet_mask.reshape(8, LANES)
    table = jnp.asarray(_tables())
    plan = jnp.concatenate([wet, jnp.pad(send_list[0], ((0, 0), (0, LANES - GHOST)))])
    *outgoing, masked, packed = pl.pallas_call(
        send_kernel,
        out_shape=(shape(PACK, LANES),) * 5 + (shape(168, 1024), shape(PACK, 1024, dtype=I32)),
        in_specs=[ANY, VMEM],
        out_specs=(VMEM,) * 7,
        scratch_shapes=[
            pltpu.VMEM((162, 1024), F32),
            pltpu.VMEM((3, 8, LANES), I32),
            pltpu.VMEM((3, PACK, LANES), I32),
            pltpu.SemaphoreType.DMA((4,)),
        ],
        compiler_params=pltpu.CompilerParams(vmem_limit_bytes=53600 << 10),
        name="send_pack",
    )(spectra, plan)
    ghosts = [
        lax.ppermute(outgoing[k], "space", [(i, (i + o) % 32) for i in range(32)])
        for k, o in enumerate(OFFSETS)
    ]
    base, gain, wind, freq, geo, code = pl.pallas_call(
        local_kernel,
        out_shape=(
            shape(168, 1024),
            shape(168, 1024),
            shape(168, 1024),
            shape(168, LANES),
            shape(2, 8, 1024),
            shape(8, 1024, dtype=I32),
        ),
        in_specs=[VMEM] * 11,
        out_specs=(VMEM,) * 6,
        scratch_shapes=[
            pltpu.VMEM((168, LANES), F32),
            pltpu.VMEM((2, 8, 1024), F32),
            pltpu.VMEM((2, 8, LANES), F32),
            pltpu.VMEM((2 * HALF, 1024), jnp.bfloat16),
            pltpu.VMEM((256, 256), jnp.bfloat16),
            pltpu.VMEM((MATRIX_SLOTS, 1024, 256), jnp.bfloat16),
            pltpu.VMEM((MATRIX_SLOTS, 2 * HALF, 256), F32),
        ],
        compiler_params=LIMIT,
        cost_estimate=cost(20_000_000, 4_000_000),
        name="local_slots",
    )(
        masked,
        packed,
        wet,
        neighbour,
        edge_weight,
        edge_angle,
        depth_class.reshape(8, LANES),
        cg_table,
        friction.reshape(8, LANES),
        wind_dir.reshape(8, LANES),
        table,
    )
    advected, sums = pl.pallas_call(
        ghost_kernel,
        out_shape=(shape(168, 1024), shape(8, 16, LANES)),
        in_specs=[VMEM] * 12,
        out_specs=(VMEM,) * 2,
        scratch_shapes=[
            pltpu.VMEM((PACK, 3 * LANES), I32),
            pltpu.VMEM((2 * GHOST_HALF, 3 * LANES), jnp.bfloat16),
            pltpu.VMEM((LANES, 256), jnp.bfloat16),
            pltpu.VMEM((2, GHOST_SLOTS, 3 * LANES, 256), jnp.bfloat16),
            pltpu.VMEM((2, GHOST_SLOTS, 2 * GHOST_HALF, 256), F32),
        ],
        compiler_params=LIMIT,
        name="ghost_slots",
    )(*ghosts, masked, base, gain, freq, geo, code, table)
    parts = lax.all_to_all(sums, "spec", split_axis=0, concat_axis=0, tiled=True)
    result, energy = pl.pallas_call(
        source_kernel,
        out_shape=(shape(162, 1024), shape(1, LANES)),
        in_specs=[VMEM] * 4,
        out_specs=(ANY, VMEM),
        scratch_shapes=[
            pltpu.VMEM((8, LANES), F32),
            pltpu.VMEM((162, 1024), F32),
            pltpu.SemaphoreType.DMA((4,)),
        ],
        compiler_params=LIMIT,
        name="source",
    )(parts, advected, wind, freq)
    return result, energy.reshape(LANES)


def solution(mesh):
    placed = (
        P("spec", "space"),
        P("space"),
        P("space"),
        P(),
        P(None, "space"),
        P(None, "space"),
        P(None, "space"),
        P("space", None, None),
        P("space"),
        P("space"),
    )
    return jax.shard_map(
        per_device,
        mesh=mesh,
        in_specs=placed,
        out_specs=(P("spec", "space"), P(("space", "spec"))),
        check_vma=False,
    )
```

```python
import math

import numpy as np
import jax
import jax.numpy as jnp
from jax import lax
from jax.experimental import pallas as pl
from jax.experimental.pallas import tpu as pltpu
from jax.sharding import PartitionSpec as P

NDIR = 36
NFREQ = 36
GHOST = 64
LANES = 128
PACK = 88
OFFSETS = (1, 31, 2, 30, 16)
SCALE = 32767.5

_F = 0.04 * np.exp(np.arange(NFREQ) * math.log(1.1))
_KAPPA = float(0.1 / (NDIR * np.sum(0.1 * _F)))
_FTOP = float(_F[-1])


def _tables():
    angle = 2.0 * np.pi * (np.arange(72) % NDIR) / NDIR
    cosine = np.repeat(np.cos(angle)[:, None], LANES, 1)
    sine = np.repeat(np.sin(angle)[:, None], LANES, 1)
    freq = np.zeros((40, LANES))
    freq[:NFREQ] = _F[:, None]
    return np.concatenate([cosine, sine, freq]).astype(np.float32)


def lane_gather(values, index):
    return jnp.take_along_axis(values, index, axis=1, mode="promise_in_bounds")


def pick(blocks, index, bits):
    level = [lane_gather(block, index) for block in blocks]
    for bit in bits:
        level = [
            jnp.where(bit, level[i + 1], level[i]) if i + 1 < len(level) else level[i]
            for i in range(0, len(level), 2)
        ]
    return level[0]


def row8(row):
    return jnp.broadcast_to(row, (8, LANES))


def turn(angle):
    h = 0.5 * angle
    t = h * h
    s = h * (
        1.0
        + t
        * (
            -1.6666666666e-1
            + t * (8.3333331e-3 + t * (-1.98412e-4 + t * (2.75567e-6 - t * 2.4700e-8)))
        )
    )
    c = 1.0 + t * (
        -0.5
        + t * (4.16666664e-2 + t * (-1.3888883e-3 + t * (2.480065e-5 + t * (-2.75358e-7 + t * 2.065e-9))))
    )
    return 1.0 - 2.0 * s * s, 2.0 * s * c


MATRIX_SLOTS = 4
GHOST_SLOTS = 3
HALF = 176
GHOST_HALF = 192
CHUNKS = ((0, 6), (6, 11))


def send_kernel(
    x_hbm, plan_ref, o0, o1, o2, o3, o4, masked_ref, packed_ref, x_ref, code_ref,
    words_ref, sem
):
    outs = (o0, o1, o2, o3, o4)
    copies = []
    for i, (first, last) in enumerate(CHUNKS):
        for j, base in enumerate((0, PACK)):
            rows = pl.ds(base + 8 * first, min(8 * last + base, 162) - base - 8 * first)
            copies.append(
                pltpu.make_async_copy(x_hbm.at[rows, :], x_ref.at[rows, :], sem.at[2 * i + j])
            )
    for copy in copies:
        copy.start()
    me = lax.axis_index("space")
    lane = lax.broadcasted_iota(jnp.int32, (8, LANES), 1)
    low = lane < GHOST
    rows = [plan_ref[pl.ds(8 + ((me + o) & 31), 1), 0:GHOST] for o in OFFSETS]
    for q, (a, b) in enumerate(((0, 1), (2, 3), (4, 4))):
        code_ref[q] = row8(jnp.concatenate([rows[a], rows[b]], axis=1))
    wet = [row8(plan_ref[b : b + 1, :].astype(jnp.float32)) for b in range(8)]

    def load(g, b):
        lanes = slice(LANES * b, LANES * b + LANES)
        if g < 20:
            value = x_ref[8 * g : 8 * g + 8, lanes] * wet[b]
        else:
            zero = jnp.zeros((6, LANES), jnp.float32)
            value = jnp.concatenate([x_ref[160:162, lanes], zero], axis=0) * wet[b]
        masked_ref[8 * g : 8 * g + 8, lanes] = value
        return (value * SCALE + 0.5).astype(jnp.int32)

    for i, (first, last) in enumerate(CHUNKS):
        copies[2 * i].wait()
        copies[2 * i + 1].wait()
        for g in range(first, last):
            for b in range(8):
                word = load(g, b) << 16
                if g < 10:
                    word = word | load(g + 11, b)
                packed_ref[8 * g : 8 * g + 8, LANES * b : LANES * b + LANES] = word

    def gather(q, carry):
        full = code_ref[q]
        index = full & 127
        bits = [(full & (128 << i)) != 0 for i in range(3)]
        for g in range(11):
            rows = slice(8 * g, 8 * g + 8)
            words_ref[q, rows, :] = pick(
                [packed_ref[rows, LANES * b : LANES * b + LANES] for b in range(8)], index, bits
            )
        return carry

    lax.fori_loop(0, 3, gather, 0)
    for q in range(3):
        for g in range(11):
            rows = slice(8 * g, 8 * g + 8)
            word = words_ref[q, rows, :]
            top = lax.shift_right_logical(word, 16).astype(jnp.float32)
            bottom = (word & 65535).astype(jnp.float32)
            if q < 2:
                outs[2 * q][rows, :] = jnp.where(low, top, pltpu.roll(bottom, 64, 1))
                outs[2 * q + 1][rows, :] = jnp.where(low, pltpu.roll(top, 64, 1), bottom)
            else:
                outs[4][rows, :] = jnp.where(low, top, bottom)


def slots(packed, blocks, code, geo, tab_ref, lanes, bit_count, product, columns, ready):
    total = [None] * 21
    shares = [None] * 9
    for m in list(range(ready, 8)) + list(range(ready)):
        full = row8(code[m : m + 1, lanes])
        index = full & 127
        bits = [(full & (128 << i)) != 0 for i in range(bit_count)]
        wc = row8(geo[0, m : m + 1, lanes])
        ws = row8(geo[1, m : m + 1, lanes])
        share = [
            jnp.maximum(
                tab_ref[8 * r : 8 * r + 8, :] * wc + tab_ref[72 + 8 * r : 80 + 8 * r, :] * ws, 0.0
            )
            for r in range(9)
        ]
        shares = [s if t is None else t + s for t, s in zip(shares, share)]
        if m < ready:
            for h in range(21):
                half = product.shape[1] // 2
                row = 8 * h + (8 if half > HALF and h > 10 else 0)
                high = product[m, row : row + 8, columns]
                low = product[m, half + row : half + row + 8, columns]
                term = share[h % 9] * (high + low)
                total[h] = term if total[h] is None else total[h] + term
            continue
        for g in range(11):
            word = pick(
                [packed[8 * g : 8 * g + 8, LANES * s : LANES * s + LANES] for s in range(blocks)],
                index,
                bits,
            )
            for h, value in ((g, lax.shift_right_logical(word, 16)), (g + 11, word & 65535)):
                if h < 21:
                    term = share[h % 9] * value.astype(jnp.float32)
                    total[h] = term if total[h] is None else total[h] + term
    return total, shares


def split(value):
    high = value.astype(jnp.bfloat16)
    return high, (value - high.astype(jnp.float32)).astype(jnp.bfloat16)


def matrix_slots(count, code, pair, blocks, count_ref, hot_ref, parts_ref, product_ref):
    size = count_ref.shape[0]
    for m in range(count):
        entry = code[m : m + 1, pair]
        for j in range(blocks):
            wanted = (entry - size * j).astype(jnp.float32).astype(jnp.bfloat16)
            hit = count_ref[...] == jnp.broadcast_to(wanted, (size, 256))
            hot_ref[m, size * j : size * j + size, :] = jnp.where(
                hit, jnp.bfloat16(1), jnp.bfloat16(0)
            )
        product_ref[m] = jnp.dot(parts_ref[...], hot_ref[m], preferred_element_type=jnp.float32)


def local_kernel(
    x_ref,
    packed,
    wet_ref,
    nb_ref,
    ew_ref,
    ea_ref,
    dc_ref,
    cg_ref,
    fr_ref,
    wd_ref,
    tab_ref,
    base_ref,
    gain_ref,
    wind_ref,
    fc_ref,
    geo_ref,
    code_ref,
    cgx,
    wloc,
    drive_ref,
    parts_ref,
    count_ref,
    hot_ref,
    product_ref,
):
    me = lax.axis_index("space")
    spec = lax.axis_index("spec")
    par = spec & 1
    first_freq = (9 * spec) >> 1
    sign = (1 - 2 * par).astype(jnp.float32)
    entry = nb_ref[...]
    ghost = entry >= 1024
    weight = ew_ref[...] * sign
    cosine, sine = turn(ea_ref[...])
    wc = weight * cosine
    ws = weight * sine
    wloc[0] = jnp.where(ghost, 0.0, wc)
    wloc[1] = jnp.where(ghost, 0.0, ws)
    geo_ref[0] = jnp.where(ghost, wc, 0.0)
    geo_ref[1] = jnp.where(ghost, ws, 0.0)
    peer = (entry - 1024) >> 6
    off = (me - peer) & 31
    half = (off == 31) | (off == 30)
    block = jnp.where(off == 16, 2, jnp.where((off == 2) | (off == 30), 1, 0))
    code_ref[...] = (entry & 63) + jnp.where(half, 64, 0) + 128 * block
    drive4 = fr_ref[...] * (sign * 4.0 / _FTOP)
    cosine, sine = turn(wd_ref[...])
    drive_ref[0] = drive4 * cosine
    drive_ref[1] = drive4 * sine
    cgpad = [None] * 5
    fpad = [None] * 5
    for j in range(5):
        line = cg_ref[pl.ds(first_freq + j, 1), :]
        cgpad[j] = row8(jnp.concatenate([line, line, line, line], axis=1))
        fpad[j] = row8(tab_ref[pl.ds(144 + first_freq + j, 1), :])
    for g in range(21):
        comp = lax.broadcasted_iota(jnp.int32, (8, LANES), 0) + 8 * g + 18 * par
        cv, fv = cgpad[0], fpad[0]
        for j in range(1, 5):
            if 8 * g + 7 + 18 >= 36 * j:
                later = comp >= 36 * j
                cv = jnp.where(later, cgpad[j], cv)
                fv = jnp.where(later, fpad[j], fv)
        cgx[8 * g : 8 * g + 8, :] = cv
        fc_ref[8 * g : 8 * g + 8, :] = fv

    for g in range(11):
        rows = slice(16 * g, 16 * g + 16)
        for b in range(8):
            lanes = slice(LANES * b, LANES * b + LANES)
            if g < 10:
                value = x_ref[rows, lanes] * SCALE
            else:
                value = jnp.concatenate(
                    [x_ref[160:168, lanes] * SCALE, jnp.zeros((8, LANES), jnp.float32)], axis=0
                )
            parts_ref[rows, lanes], parts_ref[HALF + 16 * g : HALF + 16 * g + 16, lanes] = split(
                value
            )
    count_ref[...] = lax.broadcasted_iota(jnp.int32, (256, 256), 0).astype(jnp.bfloat16)

    def node_block(b, columns, product):
        lanes = slice(LANES * b, LANES * b + LANES)
        wet = row8(wet_ref[pl.ds(b, 1), :].astype(jnp.float32))
        cls = row8(dc_ref[pl.ds(b, 1), :])
        total, shares = slots(
            packed, 8, nb_ref, wloc, tab_ref, lanes, 3, product, columns, MATRIX_SLOTS
        )
        dcos = row8(drive_ref[0, pl.ds(b, 1), :])
        dsin = row8(drive_ref[1, pl.ds(b, 1), :])
        for g in range(21):
            rows = slice(8 * g, 8 * g + 8)
            gain = wet * lane_gather(cgx[rows, :], cls)
            gain_ref[rows, lanes] = gain
            x = x_ref[rows, lanes]
            base_ref[rows, lanes] = x + gain * (total[g] * (1.0 / SCALE) - x * shares[g % 9])
            r = 8 * (g % 9)
            drive = tab_ref[r : r + 8, :] * dcos + tab_ref[72 + r : 80 + r, :] * dsin
            wind_ref[rows, lanes] = 0.125 * jnp.maximum(fc_ref[rows, :] * drive - 1.0, 0.0)

    for p in range(4):
        hot, product = hot_ref.at[p % 2], product_ref.at[p % 2]
        pair = slice(256 * p, 256 * p + 256)
        matrix_slots(MATRIX_SLOTS, nb_ref, pair, 4, count_ref, hot, parts_ref, product)
        for k in range(2):
            node_block(2 * p + k, slice(LANES * k, LANES * k + LANES), product)


def ghost_kernel(
    g0, g1, g2, g3, g4, x_ref, base_ref, gain_ref, fc_ref, geo_ref, code_ref, tab_ref, adv_ref,
    sums_ref, packed, parts_ref, count_ref, hot_ref, product_ref
):
    low = lax.broadcasted_iota(jnp.int32, (8, LANES), 1) < GHOST
    for g in range(11):
        rows = slice(8 * g, 8 * g + 8)
        whole = [ref[rows, :].astype(jnp.int32) for ref in (g0, g1, g2, g3, g4)]
        for q in range(3):
            a = whole[2 * q]
            word = (a << 16) | pltpu.roll(a, 64, 1)
            if q < 2:
                c = whole[2 * q + 1]
                word = jnp.where(low, word, (pltpu.roll(c, 64, 1) << 16) | c)
            packed[rows, LANES * q : LANES * q + LANES] = word

    zero = jnp.zeros((8, 3 * LANES), jnp.float32)
    for h in range(2):
        for g in range(0, 11, 2):
            word = packed[8 * g : min(8 * g + 16, PACK), :]
            value = (word & 65535) if h else lax.shift_right_logical(word, 16)
            value = value.astype(jnp.float32)
            if g == 10:
                value = jnp.concatenate([value, zero], axis=0)
            first = 96 * h + 8 * g
            parts_ref[first : first + 16, :], parts_ref[
                GHOST_HALF + first : GHOST_HALF + first + 16, :
            ] = split(value)
    count_ref[...] = lax.broadcasted_iota(jnp.int32, (LANES, 256), 0).astype(jnp.bfloat16)

    for p in range(4):
        matrix_slots(
            GHOST_SLOTS,
            code_ref,
            slice(256 * p, 256 * p + 256),
            3,
            count_ref,
            hot_ref.at[p % 2],
            parts_ref,
            product_ref.at[p % 2],
        )
        for k in range(2):
            b = 2 * p + k
            columns = slice(LANES * k, LANES * k + LANES)
            lanes = slice(LANES * b, LANES * b + LANES)
            total, shares = slots(
                packed,
                3,
                code_ref,
                geo_ref,
                tab_ref,
                lanes,
                2,
                product_ref.at[p % 2],
                columns,
                GHOST_SLOTS,
            )
            energy = jnp.zeros((8, LANES), jnp.float32)
            moment = jnp.zeros((8, LANES), jnp.float32)
            for g in range(21):
                rows = slice(8 * g, 8 * g + 8)
                inflow = total[g] * (1.0 / SCALE) - x_ref[rows, lanes] * shares[g % 9]
                adv = base_ref[rows, lanes] + gain_ref[rows, lanes] * inflow
                adv_ref[rows, lanes] = adv
                freq = fc_ref[rows, :]
                term = freq * adv
                energy = energy + term
                moment = moment + freq * term
            erow = jnp.sum(energy, axis=0, keepdims=True) * _KAPPA
            mrow = jnp.sum(moment, axis=0, keepdims=True) * _KAPPA
            for r in range(8):
                sums_ref[r, b : b + 1, :] = erow
                sums_ref[r, b + 8 : b + 9, :] = mrow


OUT_ROWS = ((0, 5), (5, 10), (10, 15), (15, 21))


def source_kernel(sums_ref, adv_ref, wind_ref, fc_ref, out_hbm, energy_ref, damp, out_ref, sem):
    spec = lax.axis_index("spec")
    total = sums_ref[0]
    for r in range(1, 8):
        total = total + sums_ref[r]
    energy = total[0:8]
    moment = total[8:16]
    mean = (moment + 4e-8) / (energy + 1e-6)
    scaled = mean / 0.8
    steep = energy * (scaled * scaled) * (scaled * scaled)
    damp[...] = (0.25 * steep) * steep / mean
    mine = lax.broadcasted_iota(jnp.int32, (8, LANES), 0) == spec
    energy_ref[...] = jnp.sum(jnp.where(mine, energy, 0.0), axis=0, keepdims=True)
    rate = [row8(damp[b : b + 1, :]) for b in range(8)]
    copies = []
    for i, (first, last) in enumerate(OUT_ROWS):
        for g in range(first, last):
            n = 8 if g < 20 else 2
            rows = slice(8 * g, 8 * g + 8)
            freq = fc_ref[rows, :]
            for b in range(8):
                lanes = slice(LANES * b, LANES * b + LANES)
                value = adv_ref[rows, lanes] * jnp.exp(wind_ref[rows, lanes] - rate[b] * freq)
                out_ref[8 * g : 8 * g + n, lanes] = value[0:n]
        rows = pl.ds(8 * first, min(8 * last, 162) - 8 * first)
        copies.append(
            pltpu.make_async_copy(out_ref.at[rows, :], out_hbm.at[rows, :], sem.at[i])
        )
        copies[i].start()
    for copy in copies:
        copy.wait()


VMEM = pl.BlockSpec(memory_space=pltpu.VMEM)
ANY = pl.BlockSpec(memory_space=pl.ANY)
F32 = jnp.float32
I32 = jnp.int32


def shape(*dims, dtype=jnp.float32):
    return jax.ShapeDtypeStruct(dims, dtype)


def cost(flops, size):
    return pl.CostEstimate(flops=flops, bytes_accessed=size, transcendentals=0)


LIMIT = pltpu.CompilerParams(vmem_limit_bytes=24 << 20)


def per_device(
    spectra,
    wet_mask,
    depth_class,
    cg_table,
    neighbour,
    edge_weight,
    edge_angle,
    send_list,
    friction,
    wind_dir,
):
    wet = wet_mask.reshape(8, LANES)
    table = jnp.asarray(_tables())
    plan = jnp.concatenate([wet, jnp.pad(send_list[0], ((0, 0), (0, LANES - GHOST)))])
    *outgoing, masked, packed = pl.pallas_call(
        send_kernel,
        out_shape=(shape(PACK, LANES),) * 5 + (shape(168, 1024), shape(PACK, 1024, dtype=I32)),
        in_specs=[ANY, VMEM],
        out_specs=(VMEM,) * 7,
        scratch_shapes=[
            pltpu.VMEM((162, 1024), F32),
            pltpu.VMEM((3, 8, LANES), I32),
            pltpu.VMEM((3, PACK, LANES), I32),
            pltpu.SemaphoreType.DMA((4,)),
        ],
        compiler_params=pltpu.CompilerParams(vmem_limit_bytes=53600 << 10),
        name="send_pack",
    )(spectra, plan)
    ghosts = [
        lax.ppermute(outgoing[k], "space", [(i, (i + o) % 32) for i in range(32)])
        for k, o in enumerate(OFFSETS)
    ]
    base, gain, wind, freq, geo, code = pl.pallas_call(
        local_kernel,
        out_shape=(
            shape(168, 1024),
            shape(168, 1024),
            shape(168, 1024),
            shape(168, LANES),
            shape(2, 8, 1024),
            shape(8, 1024, dtype=I32),
        ),
        in_specs=[VMEM] * 11,
        out_specs=(VMEM,) * 6,
        scratch_shapes=[
            pltpu.VMEM((168, LANES), F32),
            pltpu.VMEM((2, 8, 1024), F32),
            pltpu.VMEM((2, 8, LANES), F32),
            pltpu.VMEM((2 * HALF, 1024), jnp.bfloat16),
            pltpu.VMEM((256, 256), jnp.bfloat16),
            pltpu.VMEM((2, MATRIX_SLOTS, 1024, 256), jnp.bfloat16),
            pltpu.VMEM((2, MATRIX_SLOTS, 2 * HALF, 256), F32),
        ],
        compiler_params=LIMIT,
        cost_estimate=cost(20_000_000, 4_000_000),
        name="local_slots",
    )(
        masked,
        packed,
        wet,
        neighbour,
        edge_weight,
        edge_angle,
        depth_class.reshape(8, LANES),
        cg_table,
        friction.reshape(8, LANES),
        wind_dir.reshape(8, LANES),
        table,
    )
    advected, sums = pl.pallas_call(
        ghost_kernel,
        out_shape=(shape(168, 1024), shape(8, 16, LANES)),
        in_specs=[VMEM] * 12,
        out_specs=(VMEM,) * 2,
        scratch_shapes=[
            pltpu.VMEM((PACK, 3 * LANES), I32),
            pltpu.VMEM((2 * GHOST_HALF, 3 * LANES), jnp.bfloat16),
            pltpu.VMEM((LANES, 256), jnp.bfloat16),
            pltpu.VMEM((2, GHOST_SLOTS, 3 * LANES, 256), jnp.bfloat16),
            pltpu.VMEM((2, GHOST_SLOTS, 2 * GHOST_HALF, 256), F32),
        ],
        compiler_params=LIMIT,
        name="ghost_slots",
    )(*ghosts, masked, base, gain, freq, geo, code, table)
    parts = lax.all_to_all(sums, "spec", split_axis=0, concat_axis=0, tiled=True)
    result, energy = pl.pallas_call(
        source_kernel,
        out_shape=(shape(162, 1024), shape(1, LANES)),
        in_specs=[VMEM] * 4,
        out_specs=(ANY, VMEM),
        scratch_shapes=[
            pltpu.VMEM((8, LANES), F32),
            pltpu.VMEM((162, 1024), F32),
            pltpu.SemaphoreType.DMA((4,)),
        ],
        compiler_params=LIMIT,
        name="source",
    )(parts, advected, wind, freq)
    return result, energy.reshape(LANES)


def solution(mesh):
    placed = (
        P("spec", "space"),
        P("space"),
        P("space"),
        P(),
        P(None, "space"),
        P(None, "space"),
        P(None, "space"),
        P("space", None, None),
        P("space"),
        P("space"),
    )
    return jax.shard_map(
        per_device,
        mesh=mesh,
        in_specs=placed,
        out_specs=(P("spec", "space"), P(("space", "spec"))),
        check_vma=False,
    )
```
